128 devices in a mesh: ctx: 16 (over z, y), head: 8 (over x, core).
Axes of the slice: x: 4, y: 4, z: 4, core: 2. Of those that a mesh axis runs over, the one named last changes fastest.
Arguments:
- queries: bfloat16 [16384, 12288], P('ctx', 'head'), may hold values from -24 to 24
- key_rows: bfloat16 [16384, 768], P('ctx'), may hold values from -6 to 6
- value_rows: bfloat16 [16384, 512], P('ctx'), may hold values from -6 to 6
- comp_key_weight: float32 [32, 768], replicated, may hold values from 0.35355338 to 0.70710677
- comp_value_weight: float32 [32, 512], replicated, may hold values from 0.17677669 to 0.53033006
- block_picks: int32 [64, 4, 16], P('ctx'), may hold values from 0 to 252, as said below
- gate_logits: float32 [16384, 3, 64], P('ctx', None, 'head'), may hold values from -6 to 6
- out_weight: bfloat16 [8192, 2560], P('head'), may hold values from -0.25 to 0.25
Outputs:
- layer_out: bfloat16 [16384, 2560], P(('ctx', 'head'))
The draws below stay inside these ranges and needn't reach their ends.
Inputs may be any that keep to these rules, and one draw needn't show every extreme that they name: `block_picks`: for each group, the lists of the 256-position query blocks held by one ctx shard name exactly 1024 / 256 distinct blocks of each earlier shard and of their own shard, and none of later shards; the own-shard blocks named are the first blocks of those query blocks. Every list names the first block of its own query block. Names may repeat within a list.
All inputs are finite; a program needn't handle non-finite values.
Results may differ from the reference program's by a relative error of at most 0.03.
Values may be sent and summed in bfloat16 or wider, within the bound.
A program may use at most 128 MiB of HBM per device.

```python
import jax
import jax.numpy as jnp
from jax import lax

HEADS = 64
GROUPS = 4
QUERY_KEY_WIDTH = 192
DV = 128
D = 2560
CBLK = 32
KBLK = 64
PICKS = 16
WINDOW = 512
QBLK = 256
TOK_DEV = 1024
TOKENS = 16384
N_HEAD = 8


def draw_queries(key, part):
    base_key = jax.random.fold_in(key, 1)
    bulk = jnp.clip(jax.random.normal(base_key, (TOKENS, HEADS * QUERY_KEY_WIDTH)), -6.0, 6.0)
    return bulk.astype(jnp.bfloat16)


def draw_key_rows(key, part):
    base_key = jax.random.fold_in(key, 2)
    bulk = jnp.clip(jax.random.normal(base_key, (TOKENS, GROUPS * QUERY_KEY_WIDTH)), -6.0, 6.0)
    return bulk.astype(jnp.bfloat16)


def draw_block_picks(key, part):
    shards = TOKENS // TOK_DEV
    lists_here = TOK_DEV // QBLK
    per_owner = TOK_DEV // KBLK
    spread = QBLK // KBLK
    filled = lists_here * (PICKS - 1)
    pool_size = shards * lists_here

    def one_list_set(pair_index):
        shard_index = pair_index // GROUPS
        pair_key = jax.random.fold_in(key, pair_index)
        first_draw = jax.random.randint(jax.random.fold_in(pair_key, 1), (shards, per_owner), 0, 2 ** 20)
        chosen = jnp.argsort(first_draw * per_owner + jnp.arange(per_owner, dtype=jnp.int32)[None, :], axis=1)[:, :lists_here]
        owners = jnp.arange(shards, dtype=jnp.int32)[:, None]
        pool_blocks = (owners * per_owner + chosen).reshape(pool_size)
        earlier = jnp.repeat(jnp.arange(shards, dtype=jnp.int32) < shard_index, lists_here)
        second_sample = jax.random.randint(jax.random.fold_in(pair_key, 2), (pool_size,), 0, 2 ** 20)
        ranking = second_sample * pool_size + jnp.arange(pool_size, dtype=jnp.int32) + jnp.where(earlier, 0, 2 ** 29)
        pool_blocks = pool_blocks[jnp.argsort(ranking)]
        firsts = (shard_index * lists_here + jnp.arange(lists_here, dtype=jnp.int32)) * spread
        pool_count = lists_here * shard_index
        slot_range = jnp.arange(filled, dtype=jnp.int32)
        others = jnp.where(pool_count > 0, pool_blocks[slot_range % jnp.maximum(pool_count, 1)], firsts[slot_range % lists_here])
        pick_lists = jnp.concatenate([firsts[:, None], others.reshape(lists_here, PICKS - 1)], axis=1)
        third_draw = jax.random.randint(jax.random.fold_in(pair_key, 3), (lists_here, PICKS), 0, 2 ** 20)
        mixing = jnp.argsort(third_draw * PICKS + jnp.arange(PICKS, dtype=jnp.int32)[None, :], axis=1)
        return jnp.take_along_axis(pick_lists, mixing, axis=1)
    all_lists = jax.vmap(one_list_set)(jnp.arange(shards * GROUPS, dtype=jnp.int32))
    return all_lists.reshape(shards, GROUPS, lists_here, PICKS).transpose(0, 2, 1, 3).reshape(TOKENS // QBLK, GROUPS, PICKS).astype(jnp.int32)


def levels(stream_key, shape, cuts, low, top_value):
    def one(axis_at, shards_of):
        heights = jax.random.uniform(jax.random.fold_in(jax.random.fold_in(stream_key, 6), axis_at), (shards_of,), jnp.float32, low / len(cuts), top_value / len(cuts))
        return jnp.repeat(jnp.exp(heights), shape[axis_at] // shards_of).reshape((-1,) + (1,) * (len(shape) - axis_at - 1))

    gain = one(*cuts[0])
    for cut in cuts[1:]:
        gain = gain * one(*cut)
    return gain


def normal_values(rng, extent, deviation, limit, split=(), kind=jnp.bfloat16):
    loudness = levels(rng, extent, split, -0.22, 0.18) if split else 1.0
    result = jax.random.normal(rng, extent, jnp.float32) * deviation * loudness
    return jnp.minimum(jnp.maximum(result, -limit), limit).astype(kind)


def setup_inputs(seed: int = 0) -> dict:
    arg_keys = jax.random.split(jax.random.key(seed), 9)
    return {
        "queries": draw_queries(jax.random.fold_in(arg_keys[8], 71), 0),
        "key_rows": draw_key_rows(jax.random.fold_in(arg_keys[8], 71), 0),
        "value_rows": normal_values(arg_keys[2], (TOKENS, GROUPS * DV), 1.0, 6.0, ((0, 16),)),
        "comp_key_weight": jnp.clip(jax.random.uniform(arg_keys[3], (CBLK, GROUPS * QUERY_KEY_WIDTH), jnp.float32, 0.35355338, 0.70710677), 0.35355338, 0.70710677),
        "comp_value_weight": jnp.clip(jax.random.uniform(arg_keys[4], (CBLK, GROUPS * DV), jnp.float32, 0.17677669, 0.53033006), 0.17677669, 0.53033006),
        "block_picks": draw_block_picks(jax.random.fold_in(arg_keys[8], 71), 0),
        "gate_logits": normal_values(arg_keys[6], (TOKENS, 3, HEADS), 1.5, 6.0, ((0, 16), (2, 8)), jnp.float32),
        "out_weight": normal_values(arg_keys[7], (HEADS * DV, D), (HEADS * DV // 16) ** -0.5, 0.25, ((0, 8),)),
    }


NEG_FILL = -1e30


def softmax_parts(scores, keep_mask):
    row_top = jnp.max(jnp.where(keep_mask, scores, NEG_FILL), axis=-1, keepdims=True)
    weights = jnp.where(keep_mask, jnp.exp(scores - row_top), 0.0)
    weight_sum = jnp.sum(weights, axis=-1)
    rounded = lax.optimization_barrier(weights.astype(jnp.bfloat16)).astype(jnp.float32)
    return rounded, weight_sum


def reference(queries, key_rows, value_rows, comp_key_weight, comp_value_weight, block_picks, gate_logits, out_weight):
    per_group = HEADS // GROUPS
    score_scale = QUERY_KEY_WIDTH ** -0.5
    key_groups = key_rows.reshape(TOKENS, GROUPS, QUERY_KEY_WIDTH)
    value_groups = value_rows.reshape(TOKENS, GROUPS, DV)
    comp_keys = jnp.sum(key_rows.reshape(TOKENS // CBLK, CBLK, GROUPS * QUERY_KEY_WIDTH).astype(jnp.float32) * comp_key_weight[None], axis=1).astype(jnp.bfloat16).reshape(TOKENS // CBLK, GROUPS, QUERY_KEY_WIDTH)
    comp_values = jnp.sum(value_rows.reshape(TOKENS // CBLK, CBLK, GROUPS * DV).astype(jnp.float32) * comp_value_weight[None], axis=1).astype(jnp.bfloat16).reshape(TOKENS // CBLK, GROUPS, DV)
    comp_ends = (jnp.arange(TOKENS // CBLK, dtype=jnp.int32) + 1) * CBLK - 1
    key_pad = jnp.concatenate([jnp.zeros((WINDOW, GROUPS, QUERY_KEY_WIDTH), jnp.bfloat16), key_groups], axis=0)
    value_pad = jnp.concatenate([jnp.zeros((WINDOW, GROUPS, DV), jnp.bfloat16), value_groups], axis=0)
    key_tiles = key_groups.reshape(TOKENS // KBLK, KBLK, GROUPS, QUERY_KEY_WIDTH).transpose(2, 0, 1, 3)
    value_tiles = value_groups.reshape(TOKENS // KBLK, KBLK, GROUPS, DV).transpose(2, 0, 1, 3)
    gates = jax.nn.sigmoid(gate_logits)
    group_column = jnp.arange(GROUPS, dtype=jnp.int32)[:, None]
    pick_order = jnp.arange(PICKS, dtype=jnp.int32)

    def one_block(block_index):
        block_start = (block_index * QBLK).astype(jnp.int32)
        query_pos = block_start + jnp.arange(QBLK, dtype=jnp.int32)
        block_q = lax.dynamic_slice_in_dim(queries, block_start, QBLK, 0).reshape(QBLK, GROUPS, per_group, QUERY_KEY_WIDTH).astype(jnp.float32)

        comp_scores = jnp.einsum("qghc,ngc->qghn", block_q, comp_keys.astype(jnp.float32)) * score_scale
        keep_mask = (comp_ends[None, :] <= query_pos[:, None])[:, None, None, :]
        weights, weight_sum = softmax_parts(comp_scores, keep_mask)
        comp_out = jnp.einsum("qghn,ngd->qghd", weights, comp_values.astype(jnp.float32)) / jnp.maximum(weight_sum, 1.0)[..., None]

        win_keys = lax.dynamic_slice_in_dim(key_pad, block_start, WINDOW + QBLK, 0).astype(jnp.float32)
        win_values = lax.dynamic_slice_in_dim(value_pad, block_start, WINDOW + QBLK, 0).astype(jnp.float32)
        key_pos = block_start - WINDOW + jnp.arange(WINDOW + QBLK, dtype=jnp.int32)
        keep_mask = ((key_pos[None, :] >= 0) & (key_pos[None, :] <= query_pos[:, None]) & (key_pos[None, :] >= query_pos[:, None] - WINDOW))[:, None, None, :]
        win_scores = jnp.einsum("qghc,kgc->qghk", block_q, win_keys) * score_scale
        weights, weight_sum = softmax_parts(win_scores, keep_mask)
        win_out = jnp.einsum("qghk,kgd->qghd", weights, win_values) / weight_sum[..., None]

        chosen = lax.dynamic_index_in_dim(block_picks, block_index.astype(jnp.int32), 0, keepdims=False)
        sel_keys = key_tiles[group_column, chosen].reshape(GROUPS, PICKS * KBLK, QUERY_KEY_WIDTH).astype(jnp.float32)
        sel_values = value_tiles[group_column, chosen].reshape(GROUPS, PICKS * KBLK, DV).astype(jnp.float32)
        repeated = jnp.any((chosen[:, :, None] == chosen[:, None, :]) & (pick_order[None, None, :] < pick_order[None, :, None]), axis=-1)
        pick_pos = (chosen[:, :, None] * KBLK + jnp.arange(KBLK, dtype=jnp.int32)).reshape(GROUPS, PICKS * KBLK)
        live_mask = jnp.repeat(jnp.logical_not(repeated), KBLK, axis=1)
        keep_mask = ((pick_pos[None, :, :] <= query_pos[:, None, None]) & live_mask[None])[:, :, None, :]
        sel_scores = jnp.einsum("qghc,gkc->qghk", block_q, sel_keys) * score_scale
        weights, weight_sum = softmax_parts(sel_scores, keep_mask)
        sel_out = jnp.einsum("qghk,gkd->qghd", weights, sel_values) / weight_sum[..., None]

        block_gates = lax.dynamic_slice_in_dim(gates, block_start, QBLK, 0).reshape(QBLK, 3, GROUPS, per_group)
        mixed = block_gates[:, 0, :, :, None] * comp_out + block_gates[:, 1, :, :, None] * sel_out + block_gates[:, 2, :, :, None] * win_out
        return mixed.astype(jnp.bfloat16).reshape(QBLK, HEADS * DV)

    attended = lax.map(one_block, jnp.arange(TOKENS // QBLK, dtype=jnp.int32)).reshape(TOKENS, HEADS * DV)
    per_device = (HEADS // N_HEAD) * DV
    summed = jnp.zeros((TOKENS, D), jnp.float32)
    for head_portion in range(N_HEAD):
        partial_rows = jnp.dot(attended[:, head_portion * per_device:(head_portion + 1) * per_device], out_weight[head_portion * per_device:(head_portion + 1) * per_device], preferred_element_type=jnp.float32)
        summed = summed + lax.optimization_barrier(partial_rows.astype(jnp.bfloat16)).astype(jnp.float32)
    return summed.astype(jnp.bfloat16)
```

```python
import functools, math
import jax, jax.numpy as jnp
from jax import lax
from jax.experimental import pallas as pl
from jax.experimental.pallas import tpu as pltpu

QK=192; DV=128; CBLK=32; KBLK=64; PICKS=16; WINDOW=512; QBLK=256
DEAD=-1e30; FLOOR=-1e20
SCALE2=QK**-0.5*math.log2(math.e)
BF=jnp.bfloat16; F32=jnp.float32

def nt(a,b):
    return lax.dot_general(a,b,(((1,),(1,)),((),())),preferred_element_type=F32)

def branch(q,k,v,bias):
    s=nt(q,k)+bias
    top=jnp.maximum(jnp.max(s,axis=1,keepdims=True),FLOOR)
    w=jnp.exp2((s-top)*SCALE2).astype(BF)
    acc=jnp.dot(w,v,preferred_element_type=F32)
    return acc[:,:DV],acc[:,DV:]

def body(shard_ref,slot_ref,q_ref,gate_ref,bias_s_ref,own_ref,rim_ref,comp_ref,blk_ref,w_ref,o_ref,
         ke,ko,vx,ce,co,cx,se,so,sx,bw,bc,bs,att):
    qb=pl.program_id(0)
    shard=shard_ref[0]
    rows=lax.broadcasted_iota(jnp.int32,(QBLK,QBLK),0)
    cols=lax.broadcasted_iota(jnp.int32,(QBLK,QBLK),1)

    @pl.when(qb==0)
    def _():
        vx[:,DV:]=jnp.ones((vx.shape[0],DV),BF)
        cx[:,DV:]=jnp.ones((cx.shape[0],DV),BF)
        sx[:,DV:]=jnp.ones((sx.shape[0],DV),BF)
        def put(src,n,base):
            def one(i,_):
                x=src[i]
                r=pl.ds(pl.multiple_of(base+i*KBLK,KBLK),KBLK)
                ke[r,:]=x[:,:256]
                ko[r,:]=pltpu.roll(x[:,:256].astype(F32),64,1).astype(BF)
                vx[r,:DV]=x[:,256:]
                return 0
            lax.fori_loop(0,n,one,0)
        put(rim_ref,8,0)
        put(own_ref,16,WINDOW)
        def onec(i,_):
            x=comp_ref[i]
            r=pl.ds(pl.multiple_of(i*CBLK,CBLK),CBLK)
            ce[r,:]=x[:,:256]
            co[r,:]=pltpu.roll(x[:,:256].astype(F32),64,1).astype(BF)
            cx[r,:DV]=x[:,256:]
            return 0
        lax.fori_loop(0,16,onec,0)

    def ones(j,_):
        x=blk_ref[slot_ref[qb*PICKS+j]]
        r=pl.ds(pl.multiple_of(j*KBLK,KBLK),KBLK)
        se[r,:]=x[:,:256]
        so[r,:]=pltpu.roll(x[:,:256].astype(F32),64,1).astype(BF)
        sx[r,:DV]=x[:,256:]
        return 0
    lax.fori_loop(0,PICKS,ones,0)
    first=shard*1024+qb*QBLK
    b0=jnp.where(first<512,DEAD,0.0)
    b1=jnp.where(first<256,DEAD,0.0)
    bw[:,:256]=jnp.where(cols>=rows,b0,DEAD)
    bw[:,256:512]=jnp.full((QBLK,QBLK),b1)
    bw[:,512:]=jnp.where(cols<=rows,0.0,DEAD)
    rowc=lax.broadcasted_iota(jnp.int32,(QBLK,512),0)
    colc=lax.broadcasted_iota(jnp.int32,(QBLK,512),1)
    bc[...]=jnp.where(colc<32,jnp.where(colc*32+31<=qb*QBLK+rowc,0.0,DEAD),jnp.where(colc<(shard+1)*32,0.0,DEAD))
    rs=lax.broadcasted_iota(jnp.int32,(QBLK,1024),0)
    cs=lax.broadcasted_iota(jnp.int32,(QBLK,1024),1)
    bs[...]=jnp.where((cs<64)&(cs>rs),DEAD,jnp.broadcast_to(bias_s_ref[...].reshape(1,1024),(QBLK,1024)))
    gl=gate_ref[...]
    gates=1.0/(1.0+jnp.exp(-gl))
    gates=jnp.concatenate([gates,jnp.zeros((104,QBLK),F32)],axis=0).T
    wr=pl.ds(pl.multiple_of(qb*QBLK,QBLK),768)
    for h in range(8):
        off=(h//2)*384+(h%2)*128
        q=q_ref[:,off:off+256]
        K,C,S=(ko,co,so) if h%2 else (ke,ce,se)
        nc,dc=branch(q,C[...],cx[...],bc[...])
        ns,ds_=branch(q,S[...],sx[...],bs[...])
        nw,dw=branch(q,K[wr,:],vx[wr,:],bw[...])
        out=(gates[:,h:h+1]/jnp.maximum(dc,1.0))*nc+(gates[:,8+h:9+h]/ds_)*ns+(gates[:,16+h:17+h]/dw)*nw
        att[:,h*DV:(h+1)*DV]=out.astype(BF)
    o_ref[...]=jnp.dot(att[...],w_ref[...],preferred_element_type=F32).astype(BF)

def attend(shard,slots,q,gate,bias_s,own,rim,comp,blk,w):
    one=lambda shape: pl.BlockSpec(shape,lambda i,*_:(0,)*len(shape),pipeline_mode=pl.Buffered(1))
    return pl.pallas_call(body,
        grid_spec=pltpu.PrefetchScalarGridSpec(num_scalar_prefetch=2,grid=(4,),
        in_specs=[pl.BlockSpec((QBLK,1536),lambda i,*_:(i,0)),
                  pl.BlockSpec((24,QBLK),lambda i,*_:(0,i)),
                  pl.BlockSpec((None,1,1024),lambda i,*_:(i,0,0)),
                  one((16,64,384)),one((8,64,384)),one((16,32,384)),one((64,64,384)),one((1024,2560))],
        out_specs=pl.BlockSpec((QBLK,2560),lambda i,*_:(i,0)),
        scratch_shapes=[pltpu.VMEM((1536,256),BF)]*3+[pltpu.VMEM((512,256),BF)]*3+[pltpu.VMEM((1024,256),BF)]*3
          +[pltpu.VMEM((QBLK,768),F32),pltpu.VMEM((QBLK,512),F32),pltpu.VMEM((QBLK,1024),F32),pltpu.VMEM((QBLK,1024),BF)]),
        out_shape=jax.ShapeDtypeStruct((1024,2560),BF),
        compiler_params=pltpu.CompilerParams(vmem_limit_bytes=56<<20),
    )(shard,slots,q,gate,bias_s,own,rim,comp,blk,w)
import functools, math
import jax, jax.numpy as jnp
from jax import lax
from jax.experimental import pallas as pl
from jax.experimental.pallas import tpu as pltpu
MESH=pl.DeviceIdType.MESH
I32=jnp.int32

def plan(picks,shard):
    pos=lax.broadcasted_iota(I32,(4,PICKS),1)
    own=shard*16+4*lax.broadcasted_iota(I32,(4,PICKS),0)
    at=jnp.min(jnp.where(picks==own,pos,PICKS),axis=1,keepdims=True)
    p=jnp.where(pos==0,own,jnp.where(pos==at,picks[:,0:1],picks))
    row=jnp.concatenate([p[i:i+1] for i in range(4)]+[jnp.full((1,64),-1,I32)],axis=1)
    pr=jnp.broadcast_to(row,(128,128))
    pc=pr.astype(F32).T.astype(I32)
    ri=lax.broadcasted_iota(I32,(128,128),0)
    ci=lax.broadcasted_iota(I32,(128,128),1)
    one=lambda x: jnp.where(x,1.0,0.0)
    same=pr==pc
    dup=jnp.sum(one(same&(ri<ci)&((ri>>4)==(ci>>4))),axis=0,keepdims=True)
    new_r=jnp.where((jnp.sum(one(same&(ri<ci)),axis=0,keepdims=True)==0)&(ci[:1]<64),1.0,0.0)
    new_c=jnp.where((jnp.sum(one(same&(ci<ri)),axis=1,keepdims=True)==0)&(ri[:,:1]<64),1.0,0.0)
    mates=(pr>>4)==(pc>>4)
    rank_r=jnp.sum(jnp.where(mates&(pc<pr),new_c,0.0),axis=0,keepdims=True).astype(I32)
    rank_c=jnp.sum(jnp.where(mates&(pr<pc),new_r,0.0),axis=1,keepdims=True).astype(I32)
    slot_r=(row>>4)*4+rank_r
    slot_c=(pc[:,:1]>>4)*4+rank_c
    req=jnp.sum(jnp.where(slot_c==ci,new_c,0.0)*(pc&15).astype(F32),axis=0,keepdims=True).astype(I32)
    dead=jnp.where((dup>0)|(row>shard*16+4*(ci[:1]>>4))|(ci[:1]>=64),1.0,0.0)
    return req,slot_r,dead

def exch(picks_ref,key_ref,val_ref,kw_ref,vw_ref,
         slot_out,bias_out,own_out,rim_out,comp_out,blk_out,
         kbuf,vbuf,pk,crow,zero,reqb,reqin,send,reqs,
         ksem,lsem,rq_s,rq_r,rim_s,rim_r,cp_s,cp_r,bk_s,bk_r,sm_s):
    me=lax.axis_index("ctx"); g=lax.axis_index("head")//2
    n=16
    bar=pltpu.get_barrier_semaphore()
    def hi(i,_):
        pl.semaphore_signal(bar,inc=1,device_id={"ctx":(me+i)%n},device_id_type=MESH)
        return 0
    lax.fori_loop(1,n,hi,0)
    odd=g%2
    ck=pltpu.make_async_copy(key_ref.at[:,pl.ds(pl.multiple_of((g//2)*384,128),384)],kbuf,ksem.at[0])
    cv=pltpu.make_async_copy(val_ref.at[:,pl.ds(pl.multiple_of(g*DV,128),DV)],vbuf,ksem.at[1])
    ck.start(); cv.start()
    req,slot,dead=plan(picks_ref[:,g,:],me)
    reqb[...]=jnp.broadcast_to(req,(8,128))
    slot_out[...]=slot
    ei=lax.broadcasted_iota(I32,(128,1024),0)
    ej=lax.broadcasted_iota(I32,(128,1024),1)
    d8=jnp.broadcast_to(dead,(8,128))
    for qb in range(4):
        m=jnp.dot(d8,jnp.where(ei==qb*16+(ej>>6),1.0,0.0),preferred_element_type=F32)
        bias_out[qb]=jnp.where(m[:1]>0.5,DEAD,0.0)
    pl.semaphore_wait(bar,n-1)
    def rq(o): return pltpu.make_async_remote_copy(reqb,reqin.at[me],rq_s.at[o],rq_r.at[me],device_id={"ctx":o},device_id_type=MESH)
    def rqin(t): return pltpu.make_async_remote_copy(reqb,reqin.at[t],rq_s.at[t],rq_r.at[t],device_id={"ctx":t},device_id_type=MESH)
    lax.fori_loop(0,me,lambda o,_:(rq(o).start(),0)[1],0)
    ck.wait(); cv.wait()
    lane=lax.broadcasted_iota(I32,(KBLK,256),1)
    oddv=(lane>=0)&(lane*0+odd>0)
    keep=(lane>=odd*64)&(lane<QK+odd*64)
    kwr=kw_ref.at[:,pl.ds(pl.multiple_of((g//2)*384,128),384)]
    wk=jnp.where(oddv[:CBLK],kwr[:,128:384],kwr[:,0:256])
    wv=vw_ref[:,pl.ds(pl.multiple_of(g*DV,128),DV)]
    def pack(i,_):
        r=pl.ds(pl.multiple_of(i*KBLK,KBLK),KBLK)
        x=jnp.where(oddv,kbuf[r,128:384].astype(F32),kbuf[r,0:256].astype(F32))
        x=jnp.where(keep,x,0.0)
        x=jnp.where(oddv,pltpu.roll(x,192,1),x)
        v=vbuf[r,:]
        pk[i,:,:256]=x.astype(BF)
        pk[i,:,256:]=v
        return 0
    lax.fori_loop(0,16,pack,0)
    wk2=jnp.where(oddv[:CBLK],pltpu.roll(wk,192,1),wk)
    for b in range(32):
        r=slice((b%2)*32,(b%2)*32+32)
        crow[b:b+1,:256]=jnp.sum(pk[b//2,r,:256].astype(F32)*wk2,axis=0,keepdims=True)
        crow[b:b+1,256:]=jnp.sum(pk[b//2,r,256:].astype(F32)*wv,axis=0,keepdims=True)
    zero[...]=crow[...].astype(BF)
    def cp(t): return pltpu.make_async_remote_copy(zero,comp_out.at[t-me],cp_s.at[t-me],cp_r.at[t-me],device_id={"ctx":t},device_id_type=MESH)
    def cpin(d): return pltpu.make_async_remote_copy(zero,comp_out.at[d],cp_s.at[d],cp_r.at[d],device_id={"ctx":(me+d)%n},device_id_type=MESH)
    rim=pltpu.make_async_remote_copy(pk.at[pl.ds(8,8)],rim_out,rim_s,rim_r,device_id={"ctx":(me+1)%n},device_id_type=MESH)
    @pl.when(me<n-1)
    def _(): rim.start()
    lax.fori_loop(me+1,n,lambda t,_:(cp(t).start(),0)[1],0)
    own=pltpu.make_async_copy(pk,own_out,lsem.at[0]); own.start()
    firsts=[pltpu.make_async_copy(pk.at[4*i],blk_out.at[me*4+i],lsem.at[1+i]) for i in range(4)]
    for f in firsts: f.start()
    ownc=pltpu.make_async_copy(zero,comp_out.at[0],lsem.at[5]); ownc.start()
    def sm(t): return pltpu.make_async_copy(reqin.at[t],reqs.at[t],sm_s.at[t])
    def take(t,_):
        rqin(t).wait_recv(); sm(t).start(); return 0
    lax.fori_loop(me+1,n,take,0)
    def bk(t): return pltpu.make_async_remote_copy(send.at[t],blk_out.at[pl.ds(me*4,4)],bk_s.at[t],bk_r.at[me],device_id={"ctx":t},device_id_type=MESH)
    def bkin(o): return pltpu.make_async_remote_copy(send.at[o],blk_out.at[pl.ds(o*4,4)],bk_s.at[o],bk_r.at[o],device_id={"ctx":o},device_id_type=MESH)
    def give(t,_):
        sm(t).wait()
        for j in range(4):
            send[t,j]=pk[reqs[t,0,me*4+j]&15]
        bk(t).start()
        return 0
    lax.fori_loop(me+1,n,give,0)
    own.wait(); ownc.wait()
    for f in firsts: f.wait()
    @pl.when(me<n-1)
    def _(): rim.wait_send()
    @pl.when(me>0)
    def _(): rim.wait_recv()
    lax.fori_loop(0,me,lambda o,_:(rq(o).wait_send(),0)[1],0)
    lax.fori_loop(me+1,n,lambda t,_:(cp(t).wait_send(),0)[1],0)
    lax.fori_loop(me+1,n,lambda t,_:(bk(t).wait_send(),0)[1],0)
    lax.fori_loop(1,me+1,lambda d,_:(cpin(d).wait_recv(),0)[1],0)
    zero[...]=jnp.zeros_like(zero)
    def blank(d,_):
        c=pltpu.make_async_copy(zero,comp_out.at[d],lsem.at[6]); c.start(); c.wait(); return 0
    lax.fori_loop(me+1,n,blank,0)
    @pl.when(me==0)
    def _():
        pk[pl.ds(0,8)]=jnp.zeros((8,KBLK,384),BF)
        c=pltpu.make_async_copy(pk.at[pl.ds(0,8)],rim_out,lsem.at[6]); c.start(); c.wait()
    lax.fori_loop(0,me,lambda o,_:(bkin(o).wait_recv(),0)[1],0)

def exchange(picks,keys,vals,kw,vw):
    vm=pl.BlockSpec(memory_space=pltpu.VMEM); hb=pl.BlockSpec(memory_space=pl.ANY)
    S=jax.ShapeDtypeStruct; D=pltpu.SemaphoreType.DMA
    return pl.pallas_call(exch,
        in_specs=[vm,hb,hb,vm,vm],out_specs=[vm,vm,hb,hb,hb,hb],
        out_shape=[S((1,128),I32),S((4,1,1024),F32),S((16,64,384),BF),S((8,64,384),BF),S((16,32,384),BF),S((64,64,384),BF)],
        scratch_shapes=[pltpu.VMEM((1024,384),BF),pltpu.VMEM((1024,DV),BF),pltpu.VMEM((16,64,384),BF),pltpu.VMEM((32,384),F32),
            pltpu.VMEM((32,384),BF),pltpu.VMEM((8,128),I32),pltpu.VMEM((16,8,128),I32),pltpu.VMEM((16,4,64,384),BF),pltpu.SMEM((16,8,128),I32),
            D((2,)),D((7,)),D((16,)),D((16,)),D,D,D((16,)),D((16,)),D((16,)),D((16,)),D((16,))],
        compiler_params=pltpu.CompilerParams(collective_id=0,has_side_effects=True,vmem_limit_bytes=40<<20),
    )(picks,keys,vals,kw,vw)

def local(queries,key_rows,value_rows,kw,vw,picks,gate,w):
    shard=lax.axis_index("ctx").reshape(1)
    slot,bias,own,rim,comp,blk=exchange(picks,key_rows,value_rows,kw,vw)
    part=attend(shard,slot[0,:64],queries,gate.transpose(1,2,0).reshape(24,1024),bias,own,rim,comp,blk,w)
    return lax.psum_scatter(part,"head",scatter_dimension=0,tiled=True)

from jax.sharding import PartitionSpec as P
def solution(mesh):
    placed=(P("ctx","head"),P("ctx",None),P("ctx",None),P(),P(),P("ctx",None,None),P("ctx",None,"head"),P("head",None))
    return jax.shard_map(local,mesh=mesh,in_specs=placed,out_specs=P(("ctx","head"),None),check_vma=False)
```

```python
import math

import jax
import jax.numpy as jnp
from jax import lax
from jax.experimental import pallas as pl
from jax.experimental.pallas import tpu as pltpu
from jax.sharding import PartitionSpec as P

QK = 192
DV = 128
CBLK = 32
KBLK = 64
PICKS = 16
WINDOW = 512
QBLK = 256
N_CTX = 16
DEAD = -1e30
FLOOR = -1e20
SCALE2 = QK**-0.5 * math.log2(math.e)
BF = jnp.bfloat16
F32 = jnp.float32
I32 = jnp.int32
MESH = pl.DeviceIdType.MESH
HALF = 1280


def one(x):
    return jnp.where(x, 1.0, 0.0)


def iota(shape, axis):
    return lax.broadcasted_iota(I32, shape, axis)


def plan(picks, shard):
    pos = iota((4, PICKS), 1)
    own = shard * 16 + 4 * iota((4, PICKS), 0)
    at = jnp.min(jnp.where(picks == own, pos, PICKS), axis=1, keepdims=True)
    p = jnp.where(pos == 0, own, jnp.where(pos == at, picks[:, 0:1], picks))
    row = jnp.concatenate([p[i : i + 1] for i in range(4)] + [jnp.full((1, 64), -1, I32)], axis=1)
    pr = jnp.broadcast_to(row, (128, 128))
    pc = pr.astype(F32).T.astype(I32)
    ri = iota((128, 128), 0)
    ci = iota((128, 128), 1)
    same = pr == pc
    dup = jnp.sum(one(same & (ri < ci) & ((ri >> 4) == (ci >> 4))), axis=0, keepdims=True)
    new_r = one((jnp.sum(one(same & (ri < ci)), axis=0, keepdims=True) == 0) & (ci[:1] < 64))
    new_c = one((jnp.sum(one(same & (ci < ri)), axis=1, keepdims=True) == 0) & (ri[:, :1] < 64))
    mates = (pr >> 4) == (pc >> 4)
    rank_r = jnp.sum(jnp.where(mates & (pc < pr), new_c, 0.0), axis=0, keepdims=True).astype(I32)
    rank_c = jnp.sum(jnp.where(mates & (pr < pc), new_r, 0.0), axis=1, keepdims=True).astype(I32)
    slot_r = (row >> 4) * 4 + rank_r
    slot_c = (pc[:, :1] >> 4) * 4 + rank_c
    req = jnp.sum(jnp.where(slot_c == ci, new_c, 0.0) * (pc & 15).astype(F32), axis=0, keepdims=True)
    dead = one((dup > 0) | (row > shard * 16 + 4 * (ci[:1] >> 4)) | (ci[:1] >= 64))
    return req.astype(I32), slot_r, dead


def branch(q, k, v, bias):
    s = lax.dot_general(q, k, (((1,), (1,)), ((), ())), preferred_element_type=F32) + bias
    top = jnp.maximum(jnp.max(s, axis=1, keepdims=True), FLOOR)
    w = jnp.exp2((s - top) * SCALE2).astype(BF)
    acc = jnp.dot(w, v, preferred_element_type=F32)
    return acc[:, :DV], acc[:, DV:]


def each(lo, hi, act):
    def step(i, carry):
        act(i)
        return carry

    lax.fori_loop(lo, hi, step, 0)


def layer(
    q_hbm, key_hbm, val_hbm, kw_hbm, vw_hbm, picks_hbm, gate_hbm, w_hbm, o_hbm,
    q, kbuf, vbuf, kw, vw, picks, gate, w, gt,
    pk, crow, cown, reqb, reqin, reqs, slotb, slots, send, blk, comp, rim,
    ke, ko, vx, ce, co, cx, se, so, sx, bw, bc, bs, rowb, acc, att,
    mine, psend, precv, sa, ra, sb, rb, outb,
    lsem, sm_s, rq_s, rq_r, rim_s, rim_r, cp_s, cp_r, bk_s, bk_r, fw_s, fw_r, pr_s, pr_r, a_s, a_r, b_s, b_r,
):
    me = lax.axis_index("ctx")
    head = lax.axis_index("head")
    x = head // 2
    core = head % 2
    g = x
    odd = g % 2
    n = N_CTX
    sib = {"head": x * 2 + 1 - core}
    up = {"head": ((x + 1) % 4) * 2 + core}
    down = {"head": ((x + 3) % 4) * 2 + core}

    def remote(src, dst, ss, rs, dev):
        return pltpu.make_async_remote_copy(src, dst, ss, rs, device_id=dev, device_id_type=MESH)

    bar = pltpu.get_barrier_semaphore()
    each(1, n, lambda i: pl.semaphore_signal(bar, inc=1, device_id={"ctx": (me + i) % n}, device_id_type=MESH))
    for dev in (sib, up, down):
        pl.semaphore_signal(bar, inc=1, device_id=dev, device_id_type=MESH)

    loads = [
        pltpu.make_async_copy(picks_hbm, picks, lsem.at[0]),
        pltpu.make_async_copy(key_hbm.at[:, pl.ds(pl.multiple_of((g // 2) * 384, 128), 384)], kbuf, lsem.at[1]),
        pltpu.make_async_copy(val_hbm.at[:, pl.ds(pl.multiple_of(g * DV, 128), DV)], vbuf, lsem.at[2]),
        pltpu.make_async_copy(kw_hbm.at[:, pl.ds(pl.multiple_of((g // 2) * 384, 128), 384)], kw, lsem.at[3]),
        pltpu.make_async_copy(vw_hbm.at[:, pl.ds(pl.multiple_of(g * DV, 128), DV)], vw, lsem.at[4]),
        pltpu.make_async_copy(gate_hbm, gate, lsem.at[5]),
        pltpu.make_async_copy(q_hbm, q, lsem.at[6]),
        pltpu.make_async_copy(w_hbm, w, lsem.at[7]),
    ]
    for c in loads:
        c.start()

    loads[0].wait()
    req, slot, dead = plan(picks[:, g, :], me)
    reqb[...] = jnp.broadcast_to(req, (8, 128))
    slotb[...] = jnp.broadcast_to(slot, (8, 128))
    to_s = pltpu.make_async_copy(slotb, slots, lsem.at[8])
    to_s.start()
    pl.semaphore_wait(bar, n - 1 + 3)

    def rq(o):
        return remote(reqb, reqin.at[me], rq_s.at[o], rq_r.at[me], {"ctx": o})

    def rq_in(t):
        return remote(reqb, reqin.at[t], rq_s.at[t], rq_r.at[t], {"ctx": t})

    each(0, me, lambda o: rq(o).start())

    ei = iota((128, 1024), 0)
    ej = iota((128, 1024), 1)
    d8 = jnp.broadcast_to(dead, (8, 128))
    for qb in range(4):
        m = jnp.dot(d8, one(ei == qb * 16 + (ej >> 6)), preferred_element_type=F32)
        rowb[qb] = jnp.where(m > 0.5, DEAD, 0.0)

    for c in loads[1:5]:
        c.wait()
    lane = iota((KBLK, 256), 1)
    oddv = (lane >= 0) & (lane * 0 + odd > 0)
    keep = (lane >= odd * 64) & (lane < QK + odd * 64)
    vx[:, DV:] = jnp.ones((vx.shape[0], DV), BF)
    cx[:, DV:] = jnp.ones((cx.shape[0], DV), BF)
    sx[:, DV:] = jnp.ones((sx.shape[0], DV), BF)

    def spread(block, rows, even_ref, odd_ref, v_ref):
        even_ref[rows, :] = block[:, :256]
        odd_ref[rows, :] = pltpu.roll(block[:, :256].astype(F32), 64, 1).astype(BF)
        v_ref[rows, :DV] = block[:, 256:]

    def pack(i):
        r = pl.ds(pl.multiple_of(i * KBLK, KBLK), KBLK)
        y = jnp.where(oddv, kbuf[r, 128:384].astype(F32), kbuf[r, 0:256].astype(F32))
        y = jnp.where(keep, y, 0.0)
        y = jnp.where(oddv, pltpu.roll(y, 192, 1), y).astype(BF)
        pk[i, :, :256] = y
        pk[i, :, 256:] = vbuf[r, :]
        r2 = pl.ds(pl.multiple_of(WINDOW + i * KBLK, KBLK), KBLK)
        spread(pk[i], r2, ke, ko, vx)

    each(0, 16, pack)
    rim_c = remote(pk.at[pl.ds(8, 8)], rim, rim_s, rim_r, {"ctx": (me + 1) % n})

    @pl.when(me < n - 1)
    def _():
        rim_c.start()

    wk = jnp.where(oddv[:CBLK], kw[:, 128:384], kw[:, 0:256])
    wk = jnp.where(oddv[:CBLK], pltpu.roll(wk, 192, 1), wk)
    wv = vw[...]
    for b in range(32):
        r = slice((b % 2) * 32, (b % 2) * 32 + 32)
        crow[b : b + 1, :256] = jnp.sum(pk[b // 2, r, :256].astype(F32) * wk, axis=0, keepdims=True)
        crow[b : b + 1, 256:] = jnp.sum(pk[b // 2, r, 256:].astype(F32) * wv, axis=0, keepdims=True)
    cown[...] = crow[...].astype(BF)

    def cp(t):
        return remote(cown, comp.at[t - me], cp_s.at[t - me], cp_r.at[t - me], {"ctx": t})

    def cp_in(d):
        return remote(cown, comp.at[d], cp_s.at[d], cp_r.at[d], {"ctx": (me + d) % n})

    each(me + 1, n, lambda t: cp(t).start())

    def sm(t):
        return pltpu.make_async_copy(reqin.at[t], reqs.at[t], sm_s.at[t])

    def take(t):
        rq_in(t).wait_recv()
        sm(t).start()

    each(me + 1, n, take)

    def bk(t):
        return remote(send.at[t], blk.at[pl.ds(me * 4 + 2 * core, 2)], bk_s.at[t], bk_r.at[me], {"ctx": t})

    def bk_in(o):
        return remote(send.at[o], blk.at[pl.ds(o * 4 + 2 * core, 2)], bk_s.at[o], bk_r.at[o], {"ctx": o})

    def fw(o):
        part = blk.at[pl.ds(o * 4 + 2 * core, 2)]
        return remote(part, part, fw_s.at[o], fw_r.at[o], sib)

    def fw_in(o):
        part = blk.at[pl.ds(o * 4 + 2 - 2 * core, 2)]
        return remote(part, part, fw_s.at[o], fw_r.at[o], sib)

    def give(t):
        sm(t).wait()
        for j in range(2):
            send[t, j] = pk[reqs[t, 0, me * 4 + 2 * core + j] & 15]
        bk(t).start()

    each(me + 1, n, give)

    def pass_on(o):
        bk_in(o).wait_recv()
        fw(o).start()

    loads[5].wait()
    for qb in range(4):
        sg = 1.0 / (1.0 + jnp.exp(-gate[:, qb * QBLK : (qb + 1) * QBLK]))
        gt[qb * QBLK : (qb + 1) * QBLK, :] = jnp.concatenate([sg, jnp.zeros((104, QBLK), F32)], axis=0).T
    for i in range(4):
        blk[me * 4 + i] = pk[4 * i]
    comp[0] = cown[...]

    def blank(d):
        comp[d] = jnp.zeros((CBLK, 384), BF)

    each(me + 1, n, blank)

    @pl.when(me == 0)
    def _():
        rim[...] = jnp.zeros_like(rim)

    @pl.when(me > 0)
    def _():
        rim_c.wait_recv()

    each(1, me + 1, lambda d: cp_in(d).wait_recv())
    each(0, 8, lambda i: spread(rim[i], pl.ds(pl.multiple_of(i * KBLK, KBLK), KBLK), ke, ko, vx))
    each(0, 16, lambda i: spread(comp[i], pl.ds(pl.multiple_of(i * CBLK, CBLK), CBLK), ce, co, cx))
    loads[6].wait()
    rows = iota((QBLK, QBLK), 0)
    cols = iota((QBLK, QBLK), 1)

    def near(qb):
        base = pl.multiple_of(qb * QBLK, QBLK)
        first = me * 1024 + base
        bw[:, :256] = jnp.where(cols >= rows, jnp.where(first < 512, DEAD, 0.0), DEAD)
        bw[:, 256:512] = jnp.full((QBLK, QBLK), jnp.where(first < 256, DEAD, 0.0))
        bw[:, 512:] = jnp.where(cols <= rows, 0.0, DEAD)
        rowc = iota((QBLK, 512), 0)
        colc = iota((QBLK, 512), 1)
        bc[...] = jnp.where(
            colc < 32,
            jnp.where(colc * 32 + 31 <= base + rowc, 0.0, DEAD),
            jnp.where(colc < (me + 1) * 32, 0.0, DEAD),
        )

        def pair(p):
            gr = pltpu.roll(gt[pl.ds(base, QBLK), :], 128 - 2 * p, 1)
            for par, K, C in ((0, ke, ce), (1, ko, co)):
                qh = q[pl.ds(base, QBLK), pl.ds(pl.multiple_of(p * 384 + par * 128, 128), 256)]
                nc, dc = branch(qh, C[...], cx[...], bc[...])
                nw, dw = branch(qh, K[pl.ds(base, 768), :], vx[pl.ds(base, 768), :], bw[...])
                acc[pl.ds(base, QBLK), pl.ds(pl.multiple_of(p * 256 + par * 128, 128), DV)] = (
                    gr[:, par : par + 1] / jnp.maximum(dc, 1.0)
                ) * nc + (gr[:, 16 + par : 17 + par] / dw) * nw

        each(0, 4, pair)

    def far_setup(qb):
        def put(j):
            r = pl.ds(pl.multiple_of(j * KBLK, KBLK), KBLK)
            spread(blk[slots[0, qb * PICKS + j] & 63], r, se, so, sx)

        each(0, PICKS, put)
        rs = iota((QBLK, 1024), 0)
        cs = iota((QBLK, 1024), 1)
        bs[...] = jnp.where((cs < 64) & (cs > rs), DEAD, jnp.broadcast_to(rowb[qb][0:1, :], (QBLK, 1024)))

    def far(qb, lo, hi):
        base = pl.multiple_of(qb * QBLK, QBLK)

        def pair(p):
            gr = pltpu.roll(gt[pl.ds(base, QBLK), :], 128 - 2 * p, 1)
            for par, S in ((0, se), (1, so)):
                qh = q[pl.ds(base, QBLK), pl.ds(pl.multiple_of(p * 384 + par * 128, 128), 256)]
                ns, ds = branch(qh, S[...], sx[...], bs[...])
                c = pl.ds(pl.multiple_of(p * 256 + par * 128, 128), DV)
                att[:, c] = (acc[pl.ds(base, QBLK), c] + (gr[:, 8 + par : 9 + par] / ds) * ns).astype(BF)

        each(lo, hi, pair)

    def pr(r):
        return remote(psend.at[r], precv.at[r], pr_s.at[r], pr_r.at[r], sib)

    def project(r):
        keep_rows = pl.ds(pl.multiple_of(core * 128, 128), 128)
        give_rows = pl.ds(pl.multiple_of(128 - core * 128, 128), 128)
        a = att[give_rows, :]
        b = att[keep_rows, :]

        def tile(i):
            c = pl.ds(pl.multiple_of(i * 256, 256), 256)
            psend[r, :, c] = jnp.dot(a, w[:, c], preferred_element_type=F32).astype(BF)
            mine[r, :, c] = jnp.dot(b, w[:, c], preferred_element_type=F32)

        each(0, 10, tile)
        pr(r).start()

    A = slice(0, HALF)
    B = slice(HALF, 2 * HALF)

    def total(r, c):
        return mine[r, :, c] + precv[r, :, c].astype(F32)

    def hop_a(k):
        return remote(sa.at[k], ra.at[k], a_s.at[k], a_r.at[k], up)

    def hop_b(k):
        return remote(sb.at[k], rb.at[k], b_s.at[k], b_r.at[k], down)

    order = [(x + 3) % 4, (x + 1) % 4, (x + 2) % 4, x]
    each(0, 2, lambda r: near(jnp.where(r == 0, order[0], order[1])))
    half = me // 2
    each(half, me, pass_on)
    near(order[2])
    each(0, half, pass_on)
    loads[7].wait()
    to_s.wait()
    each(0, me, lambda o: fw_in(o).wait_recv())

    far_setup(order[0])
    far(order[0], 0, 4)
    project(0)
    far_setup(order[1])
    far(order[1], 0, 2)
    pr(0).wait_recv()
    sa[0] = total(0, A).astype(BF)
    hop_a(0).start()
    far(order[1], 2, 4)
    project(1)
    far_setup(order[2])
    far(order[2], 0, 2)
    pr(1).wait_recv()
    sb[0] = total(1, B).astype(BF)
    hop_b(0).start()
    far(order[2], 2, 4)
    project(2)
    near(order[3])
    pr(2).wait_recv()
    hop_a(0).wait_recv()
    sa[1] = (total(2, A) + ra[0].astype(F32)).astype(BF)
    hop_a(1).start()
    hop_b(0).wait_recv()
    sb[1] = (total(2, B) + rb[0].astype(F32)).astype(BF)
    hop_b(1).start()
    far_setup(order[3])
    far(order[3], 0, 4)
    hop_a(1).wait_recv()
    sa[2] = (total(1, A) + ra[1].astype(F32)).astype(BF)
    hop_a(2).start()
    hop_b(1).wait_recv()
    sb[2] = (total(0, B) + rb[1].astype(F32)).astype(BF)
    hop_b(2).start()
    project(3)
    pr(3).wait_recv()
    hop_a(2).wait_recv()
    outb[:, A] = (total(3, A) + ra[2].astype(F32)).astype(BF)
    hop_b(2).wait_recv()
    outb[:, B] = (total(3, B) + rb[2].astype(F32)).astype(BF)
    done = pltpu.make_async_copy(outb, o_hbm, lsem.at[9])
    done.start()

    each(0, me, lambda o: rq(o).wait_send())
    each(me + 1, n, lambda t: cp(t).wait_send())
    each(me + 1, n, lambda t: bk(t).wait_send())
    each(0, me, lambda o: fw(o).wait_send())

    @pl.when(me < n - 1)
    def _():
        rim_c.wait_send()

    for r in range(4):
        pr(r).wait_send()
    for k in range(3):
        hop_a(k).wait_send()
        hop_b(k).wait_send()
    done.wait()


def local(queries, key_rows, value_rows, kw, vw, picks, gate, w):
    hbm = pl.BlockSpec(memory_space=pl.ANY)
    V = pltpu.VMEM
    D = pltpu.SemaphoreType.DMA
    return pl.pallas_call(
        layer,
        in_specs=[hbm] * 8,
        out_specs=hbm,
        out_shape=jax.ShapeDtypeStruct((128, 2560), BF),
        scratch_shapes=[
            V((1024, 1536), BF), V((1024, 384), BF), V((1024, DV), BF), V((CBLK, 384), F32), V((CBLK, DV), F32),
            V((4, 4, PICKS), I32), V((24, 1024), F32), V((1024, 2560), BF), V((1024, 128), F32),
            V((16, 64, 384), BF), V((32, 384), F32), V((32, 384), BF), V((8, 128), I32), V((16, 8, 128), I32),
            pltpu.SMEM((16, 8, 128), I32), V((8, 128), I32), pltpu.SMEM((8, 128), I32),
            V((16, 2, 64, 384), BF), V((64, 64, 384), BF), V((16, 32, 384), BF), V((8, 64, 384), BF),
            V((1536, 256), BF), V((1536, 256), BF), V((1536, 256), BF),
            V((512, 256), BF), V((512, 256), BF), V((512, 256), BF),
            V((1024, 256), BF), V((1024, 256), BF), V((1024, 256), BF),
            V((QBLK, 768), F32), V((QBLK, 512), F32), V((QBLK, 1024), F32), V((4, 8, 1024), F32),
            V((1024, 1024), F32), V((QBLK, 1024), BF),
            V((4, 128, 2560), F32), V((4, 128, 2560), BF), V((4, 128, 2560), BF),
            V((3, 128, HALF), BF), V((3, 128, HALF), BF), V((3, 128, HALF), BF), V((3, 128, HALF), BF),
            V((128, 2560), BF),
            D((10,)), D((16,)), D((16,)), D((16,)), D, D, D((16,)), D((16,)), D((16,)), D((16,)), D((16,)), D((16,)),
            D((4,)), D((4,)), D((3,)), D((3,)), D((3,)), D((3,)),
        ],
        compiler_params=pltpu.CompilerParams(
            collective_id=0, has_side_effects=True, vmem_limit_bytes=60 << 20
        ),
    )(queries, key_rows, value_rows, kw, vw, picks, gate.transpose(1, 2, 0).reshape(24, 1024), w)


def solution(mesh):
    placed = (
        P("ctx", "head"), P("ctx", None), P("ctx", None), P(), P(),
        P("ctx", None, None), P("ctx", None, "head"), P("head", None),
    )
    return jax.shard_map(
        local, mesh=mesh, in_specs=placed, out_specs=P(("ctx", "head"), None), check_vma=False
    )
```

```python
import math

import jax
import jax.numpy as jnp
from jax import lax
from jax.experimental import pallas as pl
from jax.experimental.pallas import tpu as pltpu
from jax.sharding import PartitionSpec as P

QK = 192
DV = 128
CBLK = 32
KBLK = 64
PICKS = 16
WINDOW = 512
QBLK = 256
N_CTX = 16
DEAD = -1e30
FLOOR = -1e20
SCALE2 = QK**-0.5 * math.log2(math.e)
BF = jnp.bfloat16
F32 = jnp.float32
I32 = jnp.int32
MESH = pl.DeviceIdType.MESH
HALF = 1280


def one(x):
    return jnp.where(x, 1.0, 0.0)


def iota(shape, axis):
    return lax.broadcasted_iota(I32, shape, axis)


def plan(picks, shard):
    pos = iota((4, PICKS), 1)
    own = shard * 16 + 4 * iota((4, PICKS), 0)
    at = jnp.min(jnp.where(picks == own, pos, PICKS), axis=1, keepdims=True)
    p = jnp.where(pos == 0, own, jnp.where(pos == at, picks[:, 0:1], picks))
    row = jnp.concatenate([p[i : i + 1] for i in range(4)] + [jnp.full((1, 64), -1, I32)], axis=1)
    pr = jnp.broadcast_to(row, (128, 128))
    pc = pr.astype(F32).T.astype(I32)
    ri = iota((128, 128), 0)
    ci = iota((128, 128), 1)
    same = pr == pc
    dup = jnp.sum(one(same & (ri < ci) & ((ri >> 4) == (ci >> 4))), axis=0, keepdims=True)
    new_r = one((jnp.sum(one(same & (ri < ci)), axis=0, keepdims=True) == 0) & (ci[:1] < 64))
    new_c = one((jnp.sum(one(same & (ci < ri)), axis=1, keepdims=True) == 0) & (ri[:, :1] < 64))
    mates = (pr >> 4) == (pc >> 4)
    rank_r = jnp.sum(jnp.where(mates & (pc < pr), new_c, 0.0), axis=0, keepdims=True).astype(I32)
    rank_c = jnp.sum(jnp.where(mates & (pr < pc), new_r, 0.0), axis=1, keepdims=True).astype(I32)
    slot_r = (row >> 4) * 4 + rank_r
    slot_c = (pc[:, :1] >> 4) * 4 + rank_c
    req = jnp.sum(jnp.where(slot_c == ci, new_c, 0.0) * (pc & 15).astype(F32), axis=0, keepdims=True)
    dead = one((dup > 0) | (row > shard * 16 + 4 * (ci[:1] >> 4)) | (ci[:1] >= 64))
    return req.astype(I32), slot_r, dead


def branch(q, k, v, bias):
    s = lax.dot_general(q, k, (((1,), (1,)), ((), ())), preferred_element_type=F32) + bias
    top = jnp.maximum(jnp.max(s, axis=1, keepdims=True), FLOOR)
    w = jnp.exp2((s - top) * SCALE2).astype(BF)
    acc = jnp.dot(w, v, preferred_element_type=F32)
    return acc[:, :DV], acc[:, DV:]


def each(lo, hi, act):
    def step(i, carry):
        act(i)
        return carry

    lax.fori_loop(lo, hi, step, 0)


def layer(
    q_hbm, key_hbm, val_hbm, kw_hbm, vw_hbm, picks_hbm, gate_hbm, w_hbm, o_hbm,
    q, kbuf, vbuf, kw, vw, picks, gate, w, gt,
    pk, crow, cown, reqb, reqin, reqs, slotb, slots, send, blk, comp, rim,
    ke, ko, vx, ce, co, cx, se, so, sx, bw, bc, bs, rowb, acc, att,
    mine, psend, precv, sa, ra, sb, rb, outb,
    lsem, sm_s, rq_s, rq_r, rim_s, rim_r, cp_s, cp_r, bk_s, bk_r, fw_s, fw_r, pr_s, pr_r, a_s, a_r, b_s, b_r,
):
    me = lax.axis_index("ctx")
    head = lax.axis_index("head")
    x = head // 2
    core = head % 2
    g = x
    odd = g % 2
    n = N_CTX
    sib = {"head": x * 2 + 1 - core}
    up = {"head": ((x + 1) % 4) * 2 + core}
    down = {"head": ((x + 3) % 4) * 2 + core}

    def remote(src, dst, ss, rs, dev):
        return pltpu.make_async_remote_copy(src, dst, ss, rs, device_id=dev, device_id_type=MESH)

    bar = pltpu.get_barrier_semaphore()
    each(1, n, lambda i: pl.semaphore_signal(bar, inc=1, device_id={"ctx": (me + i) % n}, device_id_type=MESH))
    for dev in (sib, up, down):
        pl.semaphore_signal(bar, inc=1, device_id=dev, device_id_type=MESH)

    loads = [
        pltpu.make_async_copy(picks_hbm, picks, lsem.at[0]),
        pltpu.make_async_copy(key_hbm.at[:, pl.ds(pl.multiple_of((g // 2) * 384, 128), 384)], kbuf, lsem.at[1]),
        pltpu.make_async_copy(val_hbm.at[:, pl.ds(pl.multiple_of(g * DV, 128), DV)], vbuf, lsem.at[2]),
        pltpu.make_async_copy(kw_hbm.at[:, pl.ds(pl.multiple_of((g // 2) * 384, 128), 384)], kw, lsem.at[3]),
        pltpu.make_async_copy(vw_hbm.at[:, pl.ds(pl.multiple_of(g * DV, 128), DV)], vw, lsem.at[4]),
        pltpu.make_async_copy(gate_hbm, gate, lsem.at[5]),
        pltpu.make_async_copy(q_hbm, q, lsem.at[6]),
        pltpu.make_async_copy(w_hbm, w, lsem.at[7]),
    ]
    for c in loads:
        c.start()

    loads[0].wait()
    req, slot, dead = plan(picks[:, g, :], me)
    reqb[...] = jnp.broadcast_to(req, (8, 128))
    slotb[...] = jnp.broadcast_to(slot, (8, 128))
    to_s = pltpu.make_async_copy(slotb, slots, lsem.at[8])
    to_s.start()
    pl.semaphore_wait(bar, n - 1 + 3)

    def rq(o):
        return remote(reqb, reqin.at[me], rq_s.at[o], rq_r.at[me], {"ctx": o})

    def rq_in(t):
        return remote(reqb, reqin.at[t], rq_s.at[t], rq_r.at[t], {"ctx": t})

    each(0, me, lambda o: rq(o).start())

    ei = iota((128, 1024), 0)
    ej = iota((128, 1024), 1)
    d8 = jnp.broadcast_to(dead, (8, 128))
    for qb in range(4):
        m = jnp.dot(d8, one(ei == qb * 16 + (ej >> 6)), preferred_element_type=F32)
        rowb[qb] = jnp.where(m > 0.5, DEAD, 0.0)

    for c in loads[1:5]:
        c.wait()
    lane = iota((KBLK, 256), 1)
    oddv = (lane >= 0) & (lane * 0 + odd > 0)
    keep = (lane >= odd * 64) & (lane < QK + odd * 64)
    vx[:, DV:] = jnp.ones((vx.shape[0], DV), BF)
    cx[:, DV:] = jnp.ones((cx.shape[0], DV), BF)
    sx[:, DV:] = jnp.ones((sx.shape[0], DV), BF)

    def spread(block, rows, even_ref, odd_ref, v_ref):
        even_ref[rows, :] = block[:, :256]
        odd_ref[rows, :] = pltpu.roll(block[:, :256].astype(F32), 64, 1).astype(BF)
        v_ref[rows, :DV] = block[:, 256:]

    def pack(i):
        r = pl.ds(pl.multiple_of(i * KBLK, KBLK), KBLK)
        y = jnp.where(oddv, kbuf[r, 128:384].astype(F32), kbuf[r, 0:256].astype(F32))
        y = jnp.where(keep, y, 0.0)
        y = jnp.where(oddv, pltpu.roll(y, 192, 1), y).astype(BF)
        pk[i, :, :256] = y
        pk[i, :, 256:] = vbuf[r, :]
        r2 = pl.ds(pl.multiple_of(WINDOW + i * KBLK, KBLK), KBLK)
        spread(pk[i], r2, ke, ko, vx)

    each(0, 16, pack)
    rim_c = remote(pk.at[pl.ds(8, 8)], rim, rim_s, rim_r, {"ctx": (me + 1) % n})

    @pl.when(me < n - 1)
    def _():
        rim_c.start()

    wk = jnp.where(oddv[:CBLK], kw[:, 128:384], kw[:, 0:256])
    wk = jnp.where(oddv[:CBLK], pltpu.roll(wk, 192, 1), wk)
    wv = vw[...]
    for b in range(32):
        r = slice((b % 2) * 32, (b % 2) * 32 + 32)
        crow[b : b + 1, :256] = jnp.sum(pk[b // 2, r, :256].astype(F32) * wk, axis=0, keepdims=True)
        crow[b : b + 1, 256:] = jnp.sum(pk[b // 2, r, 256:].astype(F32) * wv, axis=0, keepdims=True)
    cown[...] = crow[...].astype(BF)

    def cp(t):
        return remote(cown, comp.at[t - me], cp_s.at[t - me], cp_r.at[t - me], {"ctx": t})

    def cp_in(d):
        return remote(cown, comp.at[d], cp_s.at[d], cp_r.at[d], {"ctx": (me + d) % n})

    each(me + 1, n, lambda t: cp(t).start())

    def sm(t):
        return pltpu.make_async_copy(reqin.at[t], reqs.at[t], sm_s.at[t])

    def take(t):
        rq_in(t).wait_recv()
        sm(t).start()

    each(me + 1, n, take)

    def bk(t):
        return remote(send.at[t], blk.at[pl.ds(me * 4 + 2 * core, 2)], bk_s.at[t], bk_r.at[me], {"ctx": t})

    def bk_in(o):
        return remote(send.at[o], blk.at[pl.ds(o * 4 + 2 * core, 2)], bk_s.at[o], bk_r.at[o], {"ctx": o})

    def fw(o):
        part = blk.at[pl.ds(o * 4 + 2 * core, 2)]
        return remote(part, part, fw_s.at[o], fw_r.at[o], sib)

    def fw_in(o):
        part = blk.at[pl.ds(o * 4 + 2 - 2 * core, 2)]
        return remote(part, part, fw_s.at[o], fw_r.at[o], sib)

    def give(t):
        sm(t).wait()
        for j in range(2):
            send[t, j] = pk[reqs[t, 0, me * 4 + 2 * core + j] & 15]
        bk(t).start()

    each(me + 1, n, give)

    def pass_on(o):
        bk_in(o).wait_recv()
        fw(o).start()

    loads[5].wait()
    for qb in range(4):
        sg = 1.0 / (1.0 + jnp.exp(-gate[:, qb * QBLK : (qb + 1) * QBLK]))
        gt[qb * QBLK : (qb + 1) * QBLK, :] = jnp.concatenate([sg, jnp.zeros((104, QBLK), F32)], axis=0).T
    for i in range(4):
        blk[me * 4 + i] = pk[4 * i]
    comp[0] = cown[...]

    def blank(d):
        comp[d] = jnp.zeros((CBLK, 384), BF)

    each(me + 1, n, blank)

    @pl.when(me == 0)
    def _():
        rim[...] = jnp.zeros_like(rim)

    @pl.when(me > 0)
    def _():
        rim_c.wait_recv()

    each(1, me + 1, lambda d: cp_in(d).wait_recv())
    each(0, 8, lambda i: spread(rim[i], pl.ds(pl.multiple_of(i * KBLK, KBLK), KBLK), ke, ko, vx))
    each(0, 16, lambda i: spread(comp[i], pl.ds(pl.multiple_of(i * CBLK, CBLK), CBLK), ce, co, cx))
    loads[6].wait()
    rows = iota((QBLK, QBLK), 0)
    cols = iota((QBLK, QBLK), 1)

    def near(qb):
        base = pl.multiple_of(qb * QBLK, QBLK)
        first = me * 1024 + base
        bw[:, :256] = jnp.where(cols >= rows, jnp.where(first < 512, DEAD, 0.0), DEAD)
        bw[:, 256:512] = jnp.full((QBLK, QBLK), jnp.where(first < 256, DEAD, 0.0))
        bw[:, 512:] = jnp.where(cols <= rows, 0.0, DEAD)
        rowc = iota((QBLK, 512), 0)
        colc = iota((QBLK, 512), 1)
        bc[...] = jnp.where(
            colc < 32,
            jnp.where(colc * 32 + 31 <= base + rowc, 0.0, DEAD),
            jnp.where(colc < (me + 1) * 32, 0.0, DEAD),
        )

        r = pl.ds(base, QBLK)
        span = pl.ds(base, 768)
        for h in range(8):
            off = (h // 2) * 384 + (h % 2) * 128
            qh = q[r, off : off + 256]
            K, C = (ko, co) if h % 2 else (ke, ce)
            nc, dc = branch(qh, C[...], cx[...], bc[...])
            nw, dw = branch(qh, K[span, :], vx[span, :], bw[...])
            acc[r, h * DV : (h + 1) * DV] = (gt[r, h : h + 1] / jnp.maximum(dc, 1.0)) * nc + (
                gt[r, 16 + h : 17 + h] / dw
            ) * nw

    def far_setup(qb):
        def put(j):
            r = pl.ds(pl.multiple_of(j * KBLK, KBLK), KBLK)
            spread(blk[slots[0, qb * PICKS + j] & 63], r, se, so, sx)

        each(0, PICKS, put)
        rs = iota((QBLK, 1024), 0)
        cs = iota((QBLK, 1024), 1)
        bs[...] = jnp.where((cs < 64) & (cs > rs), DEAD, jnp.broadcast_to(rowb[qb][0:1, :], (QBLK, 1024)))

    def far(qb):
        base = pl.multiple_of(qb * QBLK, QBLK)
        r = pl.ds(base, QBLK)
        top = pl.ds(pl.multiple_of(core * 128, 128), 128)
        low = pl.ds(pl.multiple_of(128 - core * 128, 128), 128)
        for h in range(8):
            off = (h // 2) * 384 + (h % 2) * 128
            ns, ds = branch(q[r, off : off + 256], (so if h % 2 else se)[...], sx[...], bs[...])
            c = slice(h * DV, (h + 1) * DV)
            y = (acc[r, c] + (gt[r, 8 + h : 9 + h] / ds) * ns).astype(BF)
            att[top, c] = y[:128]
            att[low, c] = y[128:]

    def pr(r, c):
        return remote(psend.at[r, c], precv.at[r, c], pr_s.at[r, c], pr_r.at[r, c], sib)

    def project(r):
        def side(i):
            c = jnp.where(r == 1, 1 - i, i)
            y = jnp.dot(att[...], w[:, pl.ds(pl.multiple_of(c * HALF, 128), HALF)], preferred_element_type=F32)
            psend[r, c] = y[128:].astype(BF)
            pr(r, c).start()
            mine[r, c] = y[:128]

        each(0, 2, side)

    A, B = 0, 1

    def total(r, c):
        pr(r, c).wait_recv()
        return mine[r, c] + precv[r, c].astype(F32)

    def hop_a(k):
        return remote(sa.at[k], ra.at[k], a_s.at[k], a_r.at[k], up)

    def hop_b(k):
        return remote(sb.at[k], rb.at[k], b_s.at[k], b_r.at[k], down)

    half = me // 2

    def block_of(r):
        return (x + jnp.where(r == 0, 3, jnp.where(r == 3, 0, r))) % 4

    def go(i):
        is_near = (i < 3) | (i == 6)
        r = jnp.where(i < 3, i, jnp.where(i < 6, i - 3, 3))

        @pl.when(i == 2)
        def _():
            each(half, me, pass_on)

        @pl.when(i == 3)
        def _():
            each(0, half, pass_on)
            loads[7].wait()
            to_s.wait()
            each(0, me, lambda o: fw_in(o).wait_recv())

        @pl.when(is_near)
        def _():
            near(block_of(r))

        @pl.when(jnp.logical_not(is_near))
        def _():
            far_setup(block_of(r))
            far(block_of(r))
            project(r)

        @pl.when(i == 3)
        def _():
            sa[0] = total(0, A).astype(BF)
            hop_a(0).start()

        @pl.when(i == 4)
        def _():
            sb[0] = total(1, B).astype(BF)
            hop_b(0).start()

        @pl.when(i == 5)
        def _():
            hop_a(0).wait_recv()
            sa[1] = (total(2, A) + ra[0].astype(F32)).astype(BF)
            hop_a(1).start()
            hop_b(0).wait_recv()
            sb[1] = (total(2, B) + rb[0].astype(F32)).astype(BF)
            hop_b(1).start()

        @pl.when(i == 6)
        def _():
            hop_a(1).wait_recv()
            sa[2] = (total(1, A) + ra[1].astype(F32)).astype(BF)
            hop_a(2).start()
            hop_b(1).wait_recv()
            sb[2] = (total(0, B) + rb[1].astype(F32)).astype(BF)
            hop_b(2).start()

    each(0, 8, go)
    own_a = total(3, A)
    hop_a(2).wait_recv()
    outb[:, :HALF] = (own_a + ra[2].astype(F32)).astype(BF)
    own_b = total(3, B)
    hop_b(2).wait_recv()
    outb[:, HALF:] = (own_b + rb[2].astype(F32)).astype(BF)
    done = pltpu.make_async_copy(outb, o_hbm, lsem.at[9])
    done.start()

    each(0, me, lambda o: rq(o).wait_send())
    each(me + 1, n, lambda t: cp(t).wait_send())
    each(me + 1, n, lambda t: bk(t).wait_send())
    each(0, me, lambda o: fw(o).wait_send())

    @pl.when(me < n - 1)
    def _():
        rim_c.wait_send()

    for r in range(4):
        pr(r, A).wait_send()
        pr(r, B).wait_send()
    for k in range(3):
        hop_a(k).wait_send()
        hop_b(k).wait_send()
    done.wait()


def local(queries, key_rows, value_rows, kw, vw, picks, gate, w):
    hbm = pl.BlockSpec(memory_space=pl.ANY)
    V = pltpu.VMEM
    D = pltpu.SemaphoreType.DMA
    return pl.pallas_call(
        layer,
        in_specs=[hbm] * 8,
        out_specs=hbm,
        out_shape=jax.ShapeDtypeStruct((128, 2560), BF),
        scratch_shapes=[
            V((1024, 1536), BF), V((1024, 384), BF), V((1024, DV), BF), V((CBLK, 384), F32), V((CBLK, DV), F32),
            V((4, 4, PICKS), I32), V((24, 1024), F32), V((1024, 2560), BF), V((1024, 128), F32),
            V((16, 64, 384), BF), V((32, 384), F32), V((32, 384), BF), V((8, 128), I32), V((16, 8, 128), I32),
            pltpu.SMEM((16, 8, 128), I32), V((8, 128), I32), pltpu.SMEM((8, 128), I32),
            V((16, 2, 64, 384), BF), V((64, 64, 384), BF), V((16, 32, 384), BF), V((8, 64, 384), BF),
            V((1536, 256), BF), V((1536, 256), BF), V((1536, 256), BF),
            V((512, 256), BF), V((512, 256), BF), V((512, 256), BF),
            V((1024, 256), BF), V((1024, 256), BF), V((1024, 256), BF),
            V((QBLK, 768), F32), V((QBLK, 512), F32), V((QBLK, 1024), F32), V((4, 8, 1024), F32),
            V((1024, 1024), F32), V((QBLK, 1024), BF),
            V((4, 2, 128, HALF), F32), V((4, 2, 128, HALF), BF), V((4, 2, 128, HALF), BF),
            V((3, 128, HALF), BF), V((3, 128, HALF), BF), V((3, 128, HALF), BF), V((3, 128, HALF), BF),
            V((128, 2560), BF),
            D((10,)), D((16,)), D((16,)), D((16,)), D, D, D((16,)), D((16,)), D((16,)), D((16,)), D((16,)), D((16,)),
            D((4, 2)), D((4, 2)), D((3,)), D((3,)), D((3,)), D((3,)),
        ],
        compiler_params=pltpu.CompilerParams(
            collective_id=0, has_side_effects=True, vmem_limit_bytes=60 << 20
        ),
    )(queries, key_rows, value_rows, kw, vw, picks, gate.transpose(1, 2, 0).reshape(24, 1024), w)


def solution(mesh):
    placed = (
        P("ctx", "head"), P("ctx", None), P("ctx", None), P(), P(),
        P("ctx", None, None), P("ctx", None, "head"), P("head", None),
    )
    return jax.shard_map(
        local, mesh=mesh, in_specs=placed, out_specs=P(("ctx", "head"), None), check_vma=False
    )
```

```python
import math

import jax
import jax.numpy as jnp
from jax import lax
from jax.experimental import pallas as pl
from jax.experimental.pallas import tpu as pltpu
from jax.sharding import PartitionSpec as P

QK = 192
DV = 128
CBLK = 32
KBLK = 64
PICKS = 16
WINDOW = 512
QBLK = 256
N_CTX = 16
DEAD = -1e30
FLOOR = -1e20
SCALE2 = QK**-0.5 * math.log2(math.e)
BF = jnp.bfloat16
F32 = jnp.float32
I32 = jnp.int32
MESH = pl.DeviceIdType.MESH
HALF = 1280


def one(x):
    return jnp.where(x, 1.0, 0.0)


def iota(shape, axis):
    return lax.broadcasted_iota(I32, shape, axis)


def plan(picks, shard):
    pos = iota((4, PICKS), 1)
    own = shard * 16 + 4 * iota((4, PICKS), 0)
    at = jnp.min(jnp.where(picks == own, pos, PICKS), axis=1, keepdims=True)
    p = jnp.where(pos == 0, own, jnp.where(pos == at, picks[:, 0:1], picks))
    row = jnp.concatenate([p[i : i + 1] for i in range(4)] + [jnp.full((1, 64), -1, I32)], axis=1)
    pr = jnp.broadcast_to(row, (128, 128))
    pc = pr.astype(F32).T.astype(I32)
    ri = iota((128, 128), 0)
    ci = iota((128, 128), 1)
    same = pr == pc
    dup = jnp.sum(one(same & (ri < ci) & ((ri >> 4) == (ci >> 4))), axis=0, keepdims=True)
    new_r = one((jnp.sum(one(same & (ri < ci)), axis=0, keepdims=True) == 0) & (ci[:1] < 64))
    new_c = one((jnp.sum(one(same & (ci < ri)), axis=1, keepdims=True) == 0) & (ri[:, :1] < 64))
    mates = (pr >> 4) == (pc >> 4)
    rank_r = jnp.sum(jnp.where(mates & (pc < pr), new_c, 0.0), axis=0, keepdims=True).astype(I32)
    rank_c = jnp.sum(jnp.where(mates & (pr < pc), new_r, 0.0), axis=1, keepdims=True).astype(I32)
    slot_r = (row >> 4) * 4 + rank_r
    slot_c = (pc[:, :1] >> 4) * 4 + rank_c
    req = jnp.sum(jnp.where(slot_c == ci, new_c, 0.0) * (pc & 15).astype(F32), axis=0, keepdims=True)
    dead = one((dup > 0) | (row > shard * 16 + 4 * (ci[:1] >> 4)) | (ci[:1] >= 64))
    return req.astype(I32), slot_r, dead


def branch(q, k, v, bias):
    s = lax.dot_general(q, k, (((1,), (1,)), ((), ())), preferred_element_type=F32) + bias
    top = jnp.maximum(jnp.max(s, axis=1, keepdims=True), FLOOR)
    w = jnp.exp2((s - top) * SCALE2).astype(BF)
    acc = jnp.dot(w, v, preferred_element_type=F32)
    return acc[:, :DV], acc[:, DV:]


def each(lo, hi, act):
    def step(i, carry):
        act(i)
        return carry

    lax.fori_loop(lo, hi, step, 0)


def layer(
    q_hbm, key_hbm, val_hbm, kw_hbm, vw_hbm, picks_hbm, gate_hbm, w_hbm, o_hbm,
    q, kbuf, vbuf, kw, vw, picks, gate, w, gt,
    pk, crow, cown, reqb, reqin, reqs, slotb, slots, send, blk, comp, rim,
    ke, ko, vx, ce, co, cx, se, so, sx, bw, bc, bs, rowb, acc, att,
    mine, psend, precv, sa, ra, sb, rb, outb,
    lsem, sm_s, rq_s, rq_r, rim_s, rim_r, cp_s, cp_r, bk_s, bk_r, fw_s, fw_r, pr_s, pr_r, a_s, a_r, b_s, b_r,
):
    me = lax.axis_index("ctx")
    head = lax.axis_index("head")
    x = head // 2
    core = head % 2
    g = x
    odd = g % 2
    n = N_CTX
    sib = {"head": x * 2 + 1 - core}
    up = {"head": ((x + 1) % 4) * 2 + core}
    down = {"head": ((x + 3) % 4) * 2 + core}

    def remote(src, dst, ss, rs, dev):
        return pltpu.make_async_remote_copy(src, dst, ss, rs, device_id=dev, device_id_type=MESH)

    bar = pltpu.get_barrier_semaphore()
    each(1, n, lambda i: pl.semaphore_signal(bar, inc=1, device_id={"ctx": (me + i) % n}, device_id_type=MESH))
    for dev in (sib, up, down):
        pl.semaphore_signal(bar, inc=1, device_id=dev, device_id_type=MESH)

    loads = [
        pltpu.make_async_copy(picks_hbm, picks, lsem.at[0]),
        pltpu.make_async_copy(key_hbm.at[:, pl.ds(pl.multiple_of((g // 2) * 384, 128), 384)], kbuf, lsem.at[1]),
        pltpu.make_async_copy(val_hbm.at[:, pl.ds(pl.multiple_of(g * DV, 128), DV)], vbuf, lsem.at[2]),
        pltpu.make_async_copy(kw_hbm.at[:, pl.ds(pl.multiple_of((g // 2) * 384, 128), 384)], kw, lsem.at[3]),
        pltpu.make_async_copy(vw_hbm.at[:, pl.ds(pl.multiple_of(g * DV, 128), DV)], vw, lsem.at[4]),
        pltpu.make_async_copy(gate_hbm, gate, lsem.at[5]),
        pltpu.make_async_copy(q_hbm, q, lsem.at[6]),
        pltpu.make_async_copy(w_hbm, w, lsem.at[7]),
    ]
    for c in loads:
        c.start()

    loads[0].wait()
    req, slot, dead = plan(picks[:, g, :], me)
    reqb[...] = jnp.broadcast_to(req, (8, 128))
    slotb[...] = jnp.broadcast_to(slot, (8, 128))
    to_s = pltpu.make_async_copy(slotb, slots, lsem.at[8])
    to_s.start()
    pl.semaphore_wait(bar, n - 1 + 3)

    def rq(o):
        return remote(reqb, reqin.at[me], rq_s.at[o], rq_r.at[me], {"ctx": o})

    def rq_in(t):
        return remote(reqb, reqin.at[t], rq_s.at[t], rq_r.at[t], {"ctx": t})

    each(0, me, lambda o: rq(o).start())

    ei = iota((128, 1024), 0)
    ej = iota((128, 1024), 1)
    d8 = jnp.broadcast_to(dead, (8, 128))
    for qb in range(4):
        m = jnp.dot(d8, one(ei == qb * 16 + (ej >> 6)), preferred_element_type=F32)
        rowb[qb] = jnp.where(m > 0.5, DEAD, 0.0)

    for c in loads[1:5]:
        c.wait()
    lane = iota((KBLK, 256), 1)
    oddv = (lane >= 0) & (lane * 0 + odd > 0)
    keep = (lane >= odd * 64) & (lane < QK + odd * 64)
    vx[:, DV:] = jnp.ones((vx.shape[0], DV), BF)
    cx[:, DV:] = jnp.ones((cx.shape[0], DV), BF)
    sx[:, DV:] = jnp.ones((sx.shape[0], DV), BF)

    def spread(block, start, n, even_ref, odd_ref, v_ref):
        r0 = pl.ds(pl.multiple_of(start, 16), n)
        r1 = pl.ds(pl.multiple_of(start + n, 16), n)
        wide = iota((n, 256), 1)
        y = jnp.where(wide < QK, block[:, 0:256].astype(F32), 0.0)
        even_ref[r0, :] = y.astype(BF)
        odd_ref[r0, :] = pltpu.roll(y, 64, 1).astype(BF)
        y = jnp.where(wide >= 64, block[:, 128:384].astype(F32), 0.0)
        odd_ref[r1, :] = y.astype(BF)
        even_ref[r1, :] = pltpu.roll(y, 192, 1).astype(BF)
        v_ref[r0, :DV] = block[:, 384:512]
        v_ref[r1, :DV] = block[:, 512:640]

    def fold(even, odd_half, v0, v1):
        return jnp.concatenate(
            [even[:, :128], even[:, 128:] + odd_half[:, :128], odd_half[:, 128:], v0, v1], axis=1
        )

    def pack(i):
        r = pl.ds(pl.multiple_of(i * KBLK, KBLK), KBLK)
        y = jnp.where(oddv, kbuf[r, 128:384].astype(F32), kbuf[r, 0:256].astype(F32))
        y = jnp.where(keep, y, 0.0)
        turned = pltpu.roll(y, 64, 1)
        back = pltpu.roll(y, 192, 1)
        even = jnp.where(oddv, back, y).astype(BF)
        odd_form = jnp.where(oddv, y, turned).astype(BF)
        v = vbuf[r, :]
        r2 = pl.ds(pl.multiple_of(WINDOW + i * KBLK, KBLK), KBLK)
        ke[r2, :] = even
        ko[r2, :] = odd_form
        vx[r2, :DV] = v
        pk[i] = fold(even[:32], odd_form[32:], v[:32], v[32:])

    for i in range(16):
        pack(i)
    rim_c = remote(
        pk.at[pl.ds(8 + 4 * core, 4)], rim.at[pl.ds(4 * core, 4)], rim_s.at[0], rim_r.at[0], {"ctx": (me + 1) % n}
    )
    rim_f = remote(rim.at[pl.ds(4 * core, 4)], rim.at[pl.ds(4 * core, 4)], rim_s.at[1], rim_r.at[1], sib)

    @pl.when(me < n - 1)
    def _():
        rim_c.start()

    wk = jnp.where(oddv[:CBLK], kw[:, 128:384], kw[:, 0:256])
    wk = jnp.where(oddv[:CBLK], pltpu.roll(wk, 192, 1), wk)
    wv = vw[...]
    for b in range(32):
        r = slice(WINDOW + b * CBLK, WINDOW + (b + 1) * CBLK)
        crow[b : b + 1, :256] = jnp.sum(ke[r, :].astype(F32) * wk, axis=0, keepdims=True)
        crow[b : b + 1, 256:] = jnp.sum(vx[r, :DV].astype(F32) * wv, axis=0, keepdims=True)
    c0 = crow[:16]
    c1 = crow[16:]
    cown[...] = fold(c0[:, :256], pltpu.roll(c1[:, :256], 64, 1), c0[:, 256:], c1[:, 256:]).astype(BF)

    def cp(t):
        return remote(cown, comp.at[t - me], cp_s.at[t - me], cp_r.at[t - me], {"ctx": t})

    def cp_in(d):
        return remote(cown, comp.at[d], cp_s.at[d], cp_r.at[d], {"ctx": (me + d) % n})

    each(me + 1, n, lambda t: cp(t).start())

    def sm(t):
        return pltpu.make_async_copy(reqin.at[t], reqs.at[t], sm_s.at[t])

    def take(t):
        rq_in(t).wait_recv()
        sm(t).start()

    each(me + 1, n, take)

    def bk(t):
        return remote(send.at[t], blk.at[pl.ds(me * 4 + 2 * core, 2)], bk_s.at[t], bk_r.at[me], {"ctx": t})

    def bk_in(o):
        return remote(send.at[o], blk.at[pl.ds(o * 4 + 2 * core, 2)], bk_s.at[o], bk_r.at[o], {"ctx": o})

    def fw(o):
        part = blk.at[pl.ds(o * 4 + 2 * core, 2)]
        return remote(part, part, fw_s.at[o], fw_r.at[o], sib)

    def fw_in(o):
        part = blk.at[pl.ds(o * 4 + 2 - 2 * core, 2)]
        return remote(part, part, fw_s.at[o], fw_r.at[o], sib)

    def give(t):
        sm(t).wait()
        for j in range(2):
            send[t, j] = pk[reqs[t, 0, me * 4 + 2 * core + j] & 15]
        bk(t).start()

    each(me + 1, n, give)

    def pass_on(o):
        bk_in(o).wait_recv()
        fw(o).start()

    loads[5].wait()
    for qb in range(4):
        sg = 1.0 / (1.0 + jnp.exp(-gate[:, qb * QBLK : (qb + 1) * QBLK]))
        gt[qb * QBLK : (qb + 1) * QBLK, :] = jnp.concatenate([sg, jnp.zeros((104, QBLK), F32)], axis=0).T
    for i in range(4):
        blk[me * 4 + i] = pk[4 * i]
    comp[0] = cown[...]

    def blank(d):
        comp[d] = jnp.zeros((16, 640), BF)

    each(me + 1, n, blank)

    @pl.when(me == 0)
    def _():
        rim[...] = jnp.zeros_like(rim)

    each(1, me + 1, lambda d: cp_in(d).wait_recv())
    for i in range(16):
        spread(comp[i], i * CBLK, 16, ce, co, cx)
    loads[6].wait()
    rows = iota((QBLK, QBLK), 0)
    cols = iota((QBLK, QBLK), 1)

    def near(qb):
        base = pl.multiple_of(qb * QBLK, QBLK)
        first = me * 1024 + base
        bw[:, :256] = jnp.where(cols >= rows, jnp.where(first < 512, DEAD, 0.0), DEAD)
        bw[:, 256:512] = jnp.full((QBLK, QBLK), jnp.where(first < 256, DEAD, 0.0))
        bw[:, 512:] = jnp.where(cols <= rows, 0.0, DEAD)
        rowc = iota((QBLK, 512), 0)
        colc = iota((QBLK, 512), 1)
        bc[...] = jnp.where(
            colc < 32,
            jnp.where(colc * 32 + 31 <= base + rowc, 0.0, DEAD),
            jnp.where(colc < (me + 1) * 32, 0.0, DEAD),
        )

        r = pl.ds(base, QBLK)
        span = pl.ds(base, 768)
        for h in range(8):
            off = (h // 2) * 384 + (h % 2) * 128
            qh = q[r, off : off + 256]
            K, C = (ko, co) if h % 2 else (ke, ce)
            nc, dc = branch(qh, C[...], cx[...], bc[...])
            nw, dw = branch(qh, K[span, :], vx[span, :], bw[...])
            acc[r, h * DV : (h + 1) * DV] = (gt[r, h : h + 1] / jnp.maximum(dc, 1.0)) * nc + (
                gt[r, 16 + h : 17 + h] / dw
            ) * nw

    def far_setup(qb):
        for j in range(PICKS):
            spread(blk[slots[0, qb * PICKS + j] & 63], j * KBLK, 32, se, so, sx)
        rs = iota((QBLK, 1024), 0)
        cs = iota((QBLK, 1024), 1)
        bs[...] = jnp.where((cs < 64) & (cs > rs), DEAD, jnp.broadcast_to(rowb[qb][0:1, :], (QBLK, 1024)))

    def far(qb):
        base = pl.multiple_of(qb * QBLK, QBLK)
        r = pl.ds(base, QBLK)
        top = pl.ds(pl.multiple_of(core * 128, 128), 128)
        low = pl.ds(pl.multiple_of(128 - core * 128, 128), 128)
        for h in range(8):
            off = (h // 2) * 384 + (h % 2) * 128
            ns, ds = branch(q[r, off : off + 256], (so if h % 2 else se)[...], sx[...], bs[...])
            c = slice(h * DV, (h + 1) * DV)
            y = (acc[r, c] + (gt[r, 8 + h : 9 + h] / ds) * ns).astype(BF)
            att[top, c] = y[:128]
            att[low, c] = y[128:]

    def pr(r, c):
        return remote(psend.at[r, c], precv.at[r, c], pr_s.at[r, c], pr_r.at[r, c], sib)

    def project(r):
        def side(i):
            c = jnp.where(r == 1, 1 - i, i)
            y = jnp.dot(att[...], w[:, pl.ds(pl.multiple_of(c * HALF, 128), HALF)], preferred_element_type=F32)
            psend[r, c] = y[128:].astype(BF)
            pr(r, c).start()
            mine[r, c] = y[:128]

        each(0, 2, side)

    A, B = 0, 1

    def total(r, c):
        pr(r, c).wait_recv()
        return mine[r, c] + precv[r, c].astype(F32)

    def hop_a(k):
        return remote(sa.at[k], ra.at[k], a_s.at[k], a_r.at[k], up)

    def hop_b(k):
        return remote(sb.at[k], rb.at[k], b_s.at[k], b_r.at[k], down)

    half = me // 2

    def block_of(r):
        return (x + jnp.where(r == 0, 2, jnp.where(r == 1, 1, jnp.where(r == 2, 3, 0)))) % 4

    def go(i):
        is_near = (i < 3) | (i == 6)
        r = jnp.where(i < 6, i - 3, 3)
        late = jnp.where(x >= 3 - i, 2 - i, 3 - i)
        near_block = jnp.where(i < 3, late, x)

        @pl.when(i == jnp.where(x >= 2, 1, 2))
        def _():
            @pl.when(me > 0)
            def _():
                rim_c.wait_recv()
                rim_f.start()
                rim_f.wait_recv()

            for j in range(8):
                spread(rim[j], j * KBLK, 32, ke, ko, vx)

        @pl.when(i == 2)
        def _():
            each(half, me, pass_on)

        @pl.when(i == 3)
        def _():
            each(0, half, pass_on)
            loads[7].wait()
            to_s.wait()
            each(0, me, lambda o: fw_in(o).wait_recv())

        @pl.when(is_near)
        def _():
            near(near_block)

        @pl.when(jnp.logical_not(is_near))
        def _():
            far_setup(block_of(r))
            far(block_of(r))
            project(r)

        @pl.when(i == 3)
        def _():
            sa[0] = total(0, A).astype(BF)
            hop_a(0).start()
            sb[0] = total(0, B).astype(BF)
            hop_b(0).start()

        @pl.when(i == 4)
        def _():
            sa[1] = total(1, B).astype(BF)
            hop_a(1).start()
            own = total(1, A)
            hop_a(0).wait_recv()
            sa[2] = (own + ra[0].astype(F32)).astype(BF)
            hop_a(2).start()

        @pl.when(i == 5)
        def _():
            sb[1] = total(2, A).astype(BF)
            hop_b(1).start()
            own = total(2, B)
            hop_b(0).wait_recv()
            sb[2] = (own + rb[0].astype(F32)).astype(BF)
            hop_b(2).start()

    each(0, 8, go)
    own_a = total(3, A)
    hop_a(2).wait_recv()
    hop_b(1).wait_recv()
    outb[:, :HALF] = (own_a + ra[2].astype(F32) + rb[1].astype(F32)).astype(BF)
    own_b = total(3, B)
    hop_a(1).wait_recv()
    hop_b(2).wait_recv()
    outb[:, HALF:] = (own_b + ra[1].astype(F32) + rb[2].astype(F32)).astype(BF)
    done = pltpu.make_async_copy(outb, o_hbm, lsem.at[9])
    done.start()

    each(0, me, lambda o: rq(o).wait_send())
    each(me + 1, n, lambda t: cp(t).wait_send())
    each(me + 1, n, lambda t: bk(t).wait_send())
    each(0, me, lambda o: fw(o).wait_send())

    @pl.when(me < n - 1)
    def _():
        rim_c.wait_send()

    @pl.when(me > 0)
    def _():
        rim_f.wait_send()

    for r in range(4):
        pr(r, A).wait_send()
        pr(r, B).wait_send()
    for k in range(3):
        hop_a(k).wait_send()
        hop_b(k).wait_send()
    done.wait()


def local(queries, key_rows, value_rows, kw, vw, picks, gate, w):
    hbm = pl.BlockSpec(memory_space=pl.ANY)
    V = pltpu.VMEM
    D = pltpu.SemaphoreType.DMA
    return pl.pallas_call(
        layer,
        in_specs=[hbm] * 8,
        out_specs=hbm,
        out_shape=jax.ShapeDtypeStruct((128, 2560), BF),
        scratch_shapes=[
            V((1024, 1536), BF), V((1024, 384), BF), V((1024, DV), BF), V((CBLK, 384), F32), V((CBLK, DV), F32),
            V((4, 4, PICKS), I32), V((24, 1024), F32), V((1024, 2560), BF), V((1024, 128), F32),
            V((16, 32, 640), BF), V((32, 384), F32), V((16, 640), BF), V((8, 128), I32), V((16, 8, 128), I32),
            pltpu.SMEM((16, 8, 128), I32), V((8, 128), I32), pltpu.SMEM((8, 128), I32),
            V((16, 2, 32, 640), BF), V((64, 32, 640), BF), V((16, 16, 640), BF), V((8, 32, 640), BF),
            V((1536, 256), BF), V((1536, 256), BF), V((1536, 256), BF),
            V((512, 256), BF), V((512, 256), BF), V((512, 256), BF),
            V((1024, 256), BF), V((1024, 256), BF), V((1024, 256), BF),
            V((QBLK, 768), F32), V((QBLK, 512), F32), V((QBLK, 1024), F32), V((4, 8, 1024), F32),
            V((1024, 1024), F32), V((QBLK, 1024), BF),
            V((4, 2, 128, HALF), F32), V((4, 2, 128, HALF), BF), V((4, 2, 128, HALF), BF),
            V((3, 128, HALF), BF), V((3, 128, HALF), BF), V((3, 128, HALF), BF), V((3, 128, HALF), BF),
            V((128, 2560), BF),
            D((10,)), D((16,)), D((16,)), D((16,)), D((2,)), D((2,)), D((16,)), D((16,)), D((16,)), D((16,)), D((16,)), D((16,)),
            D((4, 2)), D((4, 2)), D((3,)), D((3,)), D((3,)), D((3,)),
        ],
        compiler_params=pltpu.CompilerParams(
            collective_id=0, has_side_effects=True, vmem_limit_bytes=60 << 20
        ),
    )(queries, key_rows, value_rows, kw, vw, picks, gate.transpose(1, 2, 0).reshape(24, 1024), w)


def solution(mesh):
    placed = (
        P("ctx", "head"), P("ctx", None), P("ctx", None), P(), P(),
        P("ctx", None, None), P("ctx", None, "head"), P("head", None),
    )
    return jax.shard_map(
        local, mesh=mesh, in_specs=placed, out_specs=P(("ctx", "head"), None), check_vma=False
    )
```

```python
import math

import jax
import jax.numpy as jnp
from jax import lax
from jax.experimental import pallas as pl
from jax.experimental.pallas import tpu as pltpu
from jax.sharding import PartitionSpec as P

QK = 192
DV = 128
CBLK = 32
KBLK = 64
PICKS = 16
WINDOW = 512
QBLK = 256
N_CTX = 16
DEAD = -1e30
FLOOR = -1e20
SCALE2 = QK**-0.5 * math.log2(math.e)
BF = jnp.bfloat16
F32 = jnp.float32
I32 = jnp.int32
MESH = pl.DeviceIdType.MESH
HALF = 1280


def one(x):
    return jnp.where(x, 1.0, 0.0)


def iota(shape, axis):
    return lax.broadcasted_iota(I32, shape, axis)


def plan(picks, shard):
    pos = iota((4, PICKS), 1)
    own = shard * 16 + 4 * iota((4, PICKS), 0)
    at = jnp.min(jnp.where(picks == own, pos, PICKS), axis=1, keepdims=True)
    p = jnp.where(pos == 0, own, jnp.where(pos == at, picks[:, 0:1], picks))
    row = jnp.concatenate([p[i : i + 1] for i in range(4)] + [jnp.full((1, 64), -1, I32)], axis=1)
    pr = jnp.broadcast_to(row, (128, 128))
    pc = pr.astype(F32).T.astype(I32)
    ri = iota((128, 128), 0)
    ci = iota((128, 128), 1)
    same = pr == pc
    dup = jnp.sum(one(same & (ri < ci) & ((ri >> 4) == (ci >> 4))), axis=0, keepdims=True)
    new_r = one((jnp.sum(one(same & (ri < ci)), axis=0, keepdims=True) == 0) & (ci[:1] < 64))
    new_c = one((jnp.sum(one(same & (ci < ri)), axis=1, keepdims=True) == 0) & (ri[:, :1] < 64))
    mates = (pr >> 4) == (pc >> 4)
    rank_r = jnp.sum(jnp.where(mates & (pc < pr), new_c, 0.0), axis=0, keepdims=True).astype(I32)
    rank_c = jnp.sum(jnp.where(mates & (pr < pc), new_r, 0.0), axis=1, keepdims=True).astype(I32)
    slot_r = (row >> 4) * 4 + rank_r
    slot_c = (pc[:, :1] >> 4) * 4 + rank_c
    req = jnp.sum(jnp.where(slot_c == ci, new_c, 0.0) * (pc & 15).astype(F32), axis=0, keepdims=True)
    dead = one((dup > 0) | (row > shard * 16 + 4 * (ci[:1] >> 4)) | (ci[:1] >= 64))
    return req.astype(I32), slot_r, dead


def branch(q, k, v, bias):
    s = lax.dot_general(q, k, (((1,), (1,)), ((), ())), preferred_element_type=F32) + bias
    top = jnp.maximum(jnp.max(s, axis=1, keepdims=True), FLOOR)
    w = jnp.exp2((s - top) * SCALE2).astype(BF)
    acc = jnp.dot(w, v, preferred_element_type=F32)
    return acc[:, :DV], acc[:, DV:]


def each(lo, hi, act):
    def step(i, carry):
        act(i)
        return carry

    lax.fori_loop(lo, hi, step, 0)


def layer(
    q_hbm, key_hbm, val_hbm, kw_hbm, vw_hbm, picks_hbm, gate_hbm, w_hbm, o_hbm,
    q, kbuf, vbuf, kw, vw, picks, gate, w, gt,
    pk, crow, cown, reqb, reqin, reqs, slotb, slots, send, blk, comp, rim,
    ke, ko, vx, ce, co, cx, se, so, sx, bw, bc, bs, rowb, acc, accc, att,
    mine, psend, precv, sa, ra, sb, rb, outb,
    lsem, sm_s, rq_s, rq_r, rim_s, rim_r, cp_s, cp_r, bk_s, bk_r, fw_s, fw_r, pr_s, pr_r, a_s, a_r, b_s, b_r,
):
    me = lax.axis_index("ctx")
    head = lax.axis_index("head")
    x = head // 2
    core = head % 2
    g = x
    odd = g % 2
    n = N_CTX
    sib = {"head": x * 2 + 1 - core}
    up = {"head": ((x + 1) % 4) * 2 + core}
    down = {"head": ((x + 3) % 4) * 2 + core}

    def remote(src, dst, ss, rs, dev):
        return pltpu.make_async_remote_copy(src, dst, ss, rs, device_id=dev, device_id_type=MESH)

    bar = pltpu.get_barrier_semaphore()
    each(1, n, lambda i: pl.semaphore_signal(bar, inc=1, device_id={"ctx": (me + i) % n}, device_id_type=MESH))
    for dev in (sib, up, down):
        pl.semaphore_signal(bar, inc=1, device_id=dev, device_id_type=MESH)

    loads = [
        pltpu.make_async_copy(picks_hbm, picks, lsem.at[0]),
        pltpu.make_async_copy(key_hbm.at[:, pl.ds(pl.multiple_of((g // 2) * 384, 128), 384)], kbuf, lsem.at[1]),
        pltpu.make_async_copy(val_hbm.at[:, pl.ds(pl.multiple_of(g * DV, 128), DV)], vbuf, lsem.at[2]),
        pltpu.make_async_copy(kw_hbm.at[:, pl.ds(pl.multiple_of((g // 2) * 384, 128), 384)], kw, lsem.at[3]),
        pltpu.make_async_copy(vw_hbm.at[:, pl.ds(pl.multiple_of(g * DV, 128), DV)], vw, lsem.at[4]),
        pltpu.make_async_copy(gate_hbm, gate, lsem.at[5]),
        pltpu.make_async_copy(q_hbm, q, lsem.at[6]),
        pltpu.make_async_copy(w_hbm, w, lsem.at[7]),
    ]
    for c in loads:
        c.start()

    loads[0].wait()
    req, slot, dead = plan(picks[:, g, :], me)
    reqb[...] = jnp.broadcast_to(req, (8, 128))
    slotb[...] = jnp.broadcast_to(slot, (8, 128))
    to_s = pltpu.make_async_copy(slotb, slots, lsem.at[8])
    to_s.start()
    pl.semaphore_wait(bar, n - 1 + 3)

    def rq(o):
        return remote(reqb, reqin.at[me], rq_s.at[o], rq_r.at[me], {"ctx": o})

    def rq_in(t):
        return remote(reqb, reqin.at[t], rq_s.at[t], rq_r.at[t], {"ctx": t})

    each(0, me, lambda o: rq(o).start())

    ei = iota((128, 1024), 0)
    ej = iota((128, 1024), 1)
    d8 = jnp.broadcast_to(dead, (8, 128))
    for qb in range(4):
        m = jnp.dot(d8, one(ei == qb * 16 + (ej >> 6)), preferred_element_type=F32)
        rowb[qb] = jnp.where(m > 0.5, DEAD, 0.0)

    for c in loads[1:5]:
        c.wait()
    lane = iota((KBLK, 256), 1)
    oddv = (lane >= 0) & (lane * 0 + odd > 0)
    keep = (lane >= odd * 64) & (lane < QK + odd * 64)
    vx[:, DV:] = jnp.ones((vx.shape[0], DV), BF)
    cx[:, DV:] = jnp.ones((cx.shape[0], DV), BF)
    sx[:, DV:] = jnp.ones((sx.shape[0], DV), BF)

    def spread(block, start, n, even_ref, odd_ref, v_ref):
        r0 = pl.ds(pl.multiple_of(start, 16), n)
        r1 = pl.ds(pl.multiple_of(start + n, 16), n)
        wide = iota((n, 256), 1)
        y = jnp.where(wide < QK, block[:, 0:256].astype(F32), 0.0)
        even_ref[r0, :] = y.astype(BF)
        odd_ref[r0, :] = pltpu.roll(y, 64, 1).astype(BF)
        y = jnp.where(wide >= 64, block[:, 128:384].astype(F32), 0.0)
        odd_ref[r1, :] = y.astype(BF)
        even_ref[r1, :] = pltpu.roll(y, 192, 1).astype(BF)
        v_ref[r0, :DV] = block[:, 384:512]
        v_ref[r1, :DV] = block[:, 512:640]

    def fold(even, odd_half, v0, v1):
        return jnp.concatenate(
            [even[:, :128], even[:, 128:] + odd_half[:, :128], odd_half[:, 128:], v0, v1], axis=1
        )

    def pack(i):
        r = pl.ds(pl.multiple_of(i * KBLK, KBLK), KBLK)
        y = jnp.where(oddv, kbuf[r, 128:384].astype(F32), kbuf[r, 0:256].astype(F32))
        y = jnp.where(keep, y, 0.0)
        turned = pltpu.roll(y, 64, 1)
        back = pltpu.roll(y, 192, 1)
        even = jnp.where(oddv, back, y).astype(BF)
        odd_form = jnp.where(oddv, y, turned).astype(BF)
        v = vbuf[r, :]
        r2 = pl.ds(pl.multiple_of(WINDOW + i * KBLK, KBLK), KBLK)
        ke[r2, :] = even
        ko[r2, :] = odd_form
        vx[r2, :DV] = v
        pk[i] = fold(even[:32], odd_form[32:], v[:32], v[32:])

    for i in range(16):
        pack(i)
    rim_c = remote(
        pk.at[pl.ds(8 + 4 * core, 4)], rim.at[pl.ds(4 * core, 4)], rim_s.at[0], rim_r.at[0], {"ctx": (me + 1) % n}
    )
    rim_f = remote(rim.at[pl.ds(4 * core, 4)], rim.at[pl.ds(4 * core, 4)], rim_s.at[1], rim_r.at[1], sib)

    wk = jnp.where(oddv[:CBLK], kw[:, 128:384], kw[:, 0:256])
    wk = jnp.where(oddv[:CBLK], pltpu.roll(wk, 192, 1), wk)
    wv = vw[...]
    for b in range(32):
        r = slice(WINDOW + b * CBLK, WINDOW + (b + 1) * CBLK)
        crow[b : b + 1, :256] = jnp.sum(ke[r, :].astype(F32) * wk, axis=0, keepdims=True)
        crow[b : b + 1, 256:] = jnp.sum(vx[r, :DV].astype(F32) * wv, axis=0, keepdims=True)
    c0 = crow[:16]
    c1 = crow[16:]
    cown[...] = fold(c0[:, :256], pltpu.roll(c1[:, :256], 64, 1), c0[:, 256:], c1[:, 256:]).astype(BF)

    def cp(t):
        return remote(cown, comp.at[t - me], cp_s.at[t - me], cp_r.at[t - me], {"ctx": t})

    def cp_in(d):
        return remote(cown, comp.at[d], cp_s.at[d], cp_r.at[d], {"ctx": (me + d) % n})

    each(me + 1, n, lambda t: cp(t).start())

    @pl.when(me < n - 1)
    def _():
        rim_c.start()

    def sm(t):
        return pltpu.make_async_copy(reqin.at[t], reqs.at[t], sm_s.at[t])

    def take(t):
        rq_in(t).wait_recv()
        sm(t).start()

    each(me + 1, n, take)

    def bk(t):
        return remote(send.at[t], blk.at[pl.ds(me * 4 + 2 * core, 2)], bk_s.at[t], bk_r.at[me], {"ctx": t})

    def bk_in(o):
        return remote(send.at[o], blk.at[pl.ds(o * 4 + 2 * core, 2)], bk_s.at[o], bk_r.at[o], {"ctx": o})

    def fw(o):
        part = blk.at[pl.ds(o * 4 + 2 * core, 2)]
        return remote(part, part, fw_s.at[o], fw_r.at[o], sib)

    def fw_in(o):
        part = blk.at[pl.ds(o * 4 + 2 - 2 * core, 2)]
        return remote(part, part, fw_s.at[o], fw_r.at[o], sib)

    def give(t):
        sm(t).wait()
        for j in range(2):
            send[t, j] = pk[reqs[t, 0, me * 4 + 2 * core + j] & 15]
        bk(t).start()

    each(me + 1, n, give)

    def pass_on(o):
        bk_in(o).wait_recv()
        fw(o).start()

    loads[5].wait()
    for qb in range(4):
        sg = 1.0 / (1.0 + jnp.exp(-gate[:, qb * QBLK : (qb + 1) * QBLK]))
        gt[qb * QBLK : (qb + 1) * QBLK, :] = jnp.concatenate([sg, jnp.zeros((104, QBLK), F32)], axis=0).T
    for i in range(4):
        blk[me * 4 + i] = pk[4 * i]
    comp[0] = cown[...]

    def blank(d):
        comp[d] = jnp.zeros((16, 640), BF)

    each(me + 1, n, blank)

    @pl.when(me == 0)
    def _():
        rim[...] = jnp.zeros_like(rim)

    loads[6].wait()
    rows = iota((QBLK, QBLK), 0)
    cols = iota((QBLK, QBLK), 1)

    def window(qb):
        base = pl.multiple_of(qb * QBLK, QBLK)
        first = me * 1024 + base
        bw[:, :256] = jnp.where(cols >= rows, jnp.where(first < 512, DEAD, 0.0), DEAD)
        bw[:, 256:512] = jnp.full((QBLK, QBLK), jnp.where(first < 256, DEAD, 0.0))
        bw[:, 512:] = jnp.where(cols <= rows, 0.0, DEAD)
        r = pl.ds(base, QBLK)
        span = pl.ds(base, 768)
        for h in range(8):
            off = (h // 2) * 384 + (h % 2) * 128
            nw, dw = branch(q[r, off : off + 256], (ko if h % 2 else ke)[span, :], vx[span, :], bw[...])
            acc[r, h * DV : (h + 1) * DV] = (gt[r, 16 + h : 17 + h] / dw) * nw

    def compressed(qb):
        base = pl.multiple_of(qb * QBLK, QBLK)
        rowc = iota((QBLK, 512), 0)
        colc = iota((QBLK, 512), 1)
        bc[...] = jnp.where(
            colc < 32,
            jnp.where(colc * 32 + 31 <= base + rowc, 0.0, DEAD),
            jnp.where(colc < (me + 1) * 32, 0.0, DEAD),
        )
        r = pl.ds(base, QBLK)
        for h in range(8):
            off = (h // 2) * 384 + (h % 2) * 128
            nc, dc = branch(q[r, off : off + 256], (co if h % 2 else ce)[...], cx[...], bc[...])
            accc[r, h * DV : (h + 1) * DV] = (gt[r, h : h + 1] / jnp.maximum(dc, 1.0)) * nc

    def far_setup(qb):
        for j in range(PICKS):
            spread(blk[slots[0, qb * PICKS + j] & 63], j * KBLK, 32, se, so, sx)
        rs = iota((QBLK, 1024), 0)
        cs = iota((QBLK, 1024), 1)
        bs[...] = jnp.where((cs < 64) & (cs > rs), DEAD, jnp.broadcast_to(rowb[qb][0:1, :], (QBLK, 1024)))

    def far(qb):
        base = pl.multiple_of(qb * QBLK, QBLK)
        r = pl.ds(base, QBLK)
        top = pl.ds(pl.multiple_of(core * 128, 128), 128)
        low = pl.ds(pl.multiple_of(128 - core * 128, 128), 128)
        for h in range(8):
            off = (h // 2) * 384 + (h % 2) * 128
            ns, ds = branch(q[r, off : off + 256], (so if h % 2 else se)[...], sx[...], bs[...])
            c = slice(h * DV, (h + 1) * DV)
            y = (acc[r, c] + accc[r, c] + (gt[r, 8 + h : 9 + h] / ds) * ns).astype(BF)
            att[top, c] = y[:128]
            att[low, c] = y[128:]

    def pr(r, c):
        return remote(psend.at[r, c], precv.at[r, c], pr_s.at[r, c], pr_r.at[r, c], sib)

    def project(r):
        def side(i):
            c = jnp.where(r == 1, 1 - i, i)
            y = jnp.dot(att[...], w[:, pl.ds(pl.multiple_of(c * HALF, 128), HALF)], preferred_element_type=F32)
            psend[r, c] = y[128:].astype(BF)
            pr(r, c).start()
            mine[r, c] = y[:128]

        each(0, 2, side)

    A, B = 0, 1

    def total(r, c):
        pr(r, c).wait_recv()
        return mine[r, c] + precv[r, c].astype(F32)

    def hop_a(k):
        return remote(sa.at[k], ra.at[k], a_s.at[k], a_r.at[k], up)

    def hop_b(k):
        return remote(sb.at[k], rb.at[k], b_s.at[k], b_r.at[k], down)

    def block_of(r):
        return (x + jnp.where(r == 0, 2, jnp.where(r == 1, 1, jnp.where(r == 2, 3, 0)))) % 4

    def late(k):
        return jnp.where(x >= 3 - k, 2 - k, 3 - k)

    def ship0():
        sa[0] = total(0, A).astype(BF)
        hop_a(0).start()
        sb[0] = total(0, B).astype(BF)
        hop_b(0).start()

    def ship1():
        sa[1] = total(1, B).astype(BF)
        hop_a(1).start()
        own = total(1, A)
        hop_a(0).wait_recv()
        sa[2] = (own + ra[0].astype(F32)).astype(BF)
        hop_a(2).start()

    def ship2():
        sb[1] = total(2, A).astype(BF)
        hop_b(1).start()
        own = total(2, B)
        hop_b(0).wait_recv()
        sb[2] = (own + rb[0].astype(F32)).astype(BF)
        hop_b(2).start()

    third = me // 3

    def go(i):
        is_w = (i == 0) | (i == 4) | (i == 5) | (i == 9)
        is_c = ((i >= 1) & (i <= 3)) | (i == 10)
        is_f = ((i >= 6) & (i <= 8)) | (i == 11)
        w_block = jnp.where(i == 9, x, late(jnp.where(i == 0, 0, i - 3)))
        c_block = jnp.where(i == 10, x, late(i - 1))
        r = jnp.where(i == 11, 3, i - 6)

        @pl.when(i == 1)
        def _():
            each(1, me + 1, lambda d: cp_in(d).wait_recv())
            for k in range(16):
                spread(comp[k], k * CBLK, 16, ce, co, cx)

        @pl.when(i == 4)
        def _():
            @pl.when(me > 0)
            def _():
                rim_c.wait_recv()
                rim_f.start()

            each(2 * third, me, pass_on)

            @pl.when(me > 0)
            def _():
                rim_f.wait_recv()

            for j in range(8):
                spread(rim[j], j * KBLK, 32, ke, ko, vx)

        @pl.when(i == 5)
        def _():
            each(third, 2 * third, pass_on)

        @pl.when(i == 6)
        def _():
            each(0, third, pass_on)
            loads[7].wait()
            to_s.wait()
            each(0, me, lambda o: fw_in(o).wait_recv())

        @pl.when(is_w)
        def _():
            window(w_block)

        @pl.when(is_c)
        def _():
            compressed(c_block)

        @pl.when(is_f)
        def _():
            far_setup(block_of(r))

            @pl.when(i == 7)
            def _():
                ship0()

            @pl.when(i == 8)
            def _():
                ship1()

            far(block_of(r))
            project(r)

        @pl.when(i == 8)
        def _():
            ship2()

    each(0, 12, go)
    own_a = total(3, A)
    hop_a(2).wait_recv()
    hop_b(1).wait_recv()
    outb[:, :HALF] = (own_a + ra[2].astype(F32) + rb[1].astype(F32)).astype(BF)
    own_b = total(3, B)
    hop_a(1).wait_recv()
    hop_b(2).wait_recv()
    outb[:, HALF:] = (own_b + ra[1].astype(F32) + rb[2].astype(F32)).astype(BF)
    done = pltpu.make_async_copy(outb, o_hbm, lsem.at[9])
    done.start()

    each(0, me, lambda o: rq(o).wait_send())
    each(me + 1, n, lambda t: cp(t).wait_send())
    each(me + 1, n, lambda t: bk(t).wait_send())
    each(0, me, lambda o: fw(o).wait_send())

    @pl.when(me < n - 1)
    def _():
        rim_c.wait_send()

    @pl.when(me > 0)
    def _():
        rim_f.wait_send()

    for r in range(4):
        pr(r, A).wait_send()
        pr(r, B).wait_send()
    for k in range(3):
        hop_a(k).wait_send()
        hop_b(k).wait_send()
    done.wait()


def local(queries, key_rows, value_rows, kw, vw, picks, gate, w):
    hbm = pl.BlockSpec(memory_space=pl.ANY)
    V = pltpu.VMEM
    D = pltpu.SemaphoreType.DMA
    return pl.pallas_call(
        layer,
        in_specs=[hbm] * 8,
        out_specs=hbm,
        out_shape=jax.ShapeDtypeStruct((128, 2560), BF),
        scratch_shapes=[
            V((1024, 1536), BF), V((1024, 384), BF), V((1024, DV), BF), V((CBLK, 384), F32), V((CBLK, DV), F32),
            V((4, 4, PICKS), I32), V((24, 1024), F32), V((1024, 2560), BF), V((1024, 128), F32),
            V((16, 32, 640), BF), V((32, 384), F32), V((16, 640), BF), V((8, 128), I32), V((16, 8, 128), I32),
            pltpu.SMEM((16, 8, 128), I32), V((8, 128), I32), pltpu.SMEM((8, 128), I32),
            V((16, 2, 32, 640), BF), V((64, 32, 640), BF), V((16, 16, 640), BF), V((8, 32, 640), BF),
            V((1536, 256), BF), V((1536, 256), BF), V((1536, 256), BF),
            V((512, 256), BF), V((512, 256), BF), V((512, 256), BF),
            V((1024, 256), BF), V((1024, 256), BF), V((1024, 256), BF),
            V((QBLK, 768), F32), V((QBLK, 512), F32), V((QBLK, 1024), F32), V((4, 8, 1024), F32),
            V((1024, 1024), F32), V((1024, 1024), F32), V((QBLK, 1024), BF),
            V((4, 2, 128, HALF), F32), V((4, 2, 128, HALF), BF), V((4, 2, 128, HALF), BF),
            V((3, 128, HALF), BF), V((3, 128, HALF), BF), V((3, 128, HALF), BF), V((3, 128, HALF), BF),
            V((128, 2560), BF),
            D((10,)), D((16,)), D((16,)), D((16,)), D((2,)), D((2,)), D((16,)), D((16,)), D((16,)), D((16,)), D((16,)), D((16,)),
            D((4, 2)), D((4, 2)), D((3,)), D((3,)), D((3,)), D((3,)),
        ],
        compiler_params=pltpu.CompilerParams(
            collective_id=0, has_side_effects=True, vmem_limit_bytes=60 << 20
        ),
    )(queries, key_rows, value_rows, kw, vw, picks, gate.transpose(1, 2, 0).reshape(24, 1024), w)


def solution(mesh):
    placed = (
        P("ctx", "head"), P("ctx", None), P("ctx", None), P(), P(),
        P("ctx", None, None), P("ctx", None, "head"), P("head", None),
    )
    return jax.shard_map(
        local, mesh=mesh, in_specs=placed, out_specs=P(("ctx", "head"), None), check_vma=False
    )
```

```python
import math

import jax
import jax.numpy as jnp
from jax import lax
from jax.experimental import pallas as pl
from jax.experimental.pallas import tpu as pltpu
from jax.sharding import PartitionSpec as P

QK = 192
DV = 128
CBLK = 32
KBLK = 64
PICKS = 16
WINDOW = 512
QBLK = 256
N_CTX = 16
DEAD = -1e30
FLOOR = -1e20
SCALE2 = QK**-0.5 * math.log2(math.e)
BF = jnp.bfloat16
F32 = jnp.float32
I32 = jnp.int32
MESH = pl.DeviceIdType.MESH
HALF = 1280


def one(x):
    return jnp.where(x, 1.0, 0.0)


def iota(shape, axis):
    return lax.broadcasted_iota(I32, shape, axis)


def plan(picks, shard):
    pos = iota((4, PICKS), 1)
    own = shard * 16 + 4 * iota((4, PICKS), 0)
    at = jnp.min(jnp.where(picks == own, pos, PICKS), axis=1, keepdims=True)
    p = jnp.where(pos == 0, own, jnp.where(pos == at, picks[:, 0:1], picks))
    row = jnp.concatenate([p[i : i + 1] for i in range(4)] + [jnp.full((1, 64), -1, I32)], axis=1)
    pr = jnp.broadcast_to(row, (128, 128))
    pc = pr.astype(F32).T.astype(I32)
    ri = iota((128, 128), 0)
    ci = iota((128, 128), 1)
    same = pr == pc
    dup = jnp.sum(one(same & (ri < ci) & ((ri >> 4) == (ci >> 4))), axis=0, keepdims=True)
    new_r = one((jnp.sum(one(same & (ri < ci)), axis=0, keepdims=True) == 0) & (ci[:1] < 64))
    new_c = one((jnp.sum(one(same & (ci < ri)), axis=1, keepdims=True) == 0) & (ri[:, :1] < 64))
    mates = (pr >> 4) == (pc >> 4)
    rank_r = jnp.sum(jnp.where(mates & (pc < pr), new_c, 0.0), axis=0, keepdims=True).astype(I32)
    rank_c = jnp.sum(jnp.where(mates & (pr < pc), new_r, 0.0), axis=1, keepdims=True).astype(I32)
    slot_r = (row >> 4) * 4 + rank_r
    slot_c = (pc[:, :1] >> 4) * 4 + rank_c
    req = jnp.sum(jnp.where(slot_c == ci, new_c, 0.0) * (pc & 15).astype(F32), axis=0, keepdims=True)
    dead = one((dup > 0) | (row > shard * 16 + 4 * (ci[:1] >> 4)) | (ci[:1] >= 64))
    return req.astype(I32), slot_r, dead


def branch(q, k, v, bias):
    s = lax.dot_general(q, k, (((1,), (1,)), ((), ())), preferred_element_type=F32) + bias
    top = jnp.maximum(jnp.max(s, axis=1, keepdims=True), FLOOR)
    w = jnp.exp2((s - top) * SCALE2).astype(BF)
    acc = jnp.dot(w, v, preferred_element_type=F32)
    return acc[:, :DV], acc[:, DV:]


def each(lo, hi, act):
    def step(i, carry):
        act(i)
        return carry

    lax.fori_loop(lo, hi, step, 0)


def layer(
    q_hbm, key_hbm, val_hbm, kw_hbm, vw_hbm, picks_hbm, gate_hbm, w_hbm, o_hbm,
    q, kbuf, vbuf, kw, vw, picks, gate, w, gt,
    pk, crow, cown, reqb, reqin, reqs, slotb, slots, send, blk, comp, rim,
    ke, ko, vx, ce, co, cx, se, so, sx, bw, bc, bs, rowb, acc, accc, att,
    mine, psend, precv, sa, ra, sb, rb, outb,
    lsem, sm_s, rq_s, rq_r, rim_s, rim_r, cp_s, cp_r, bk_s, bk_r, fw_s, fw_r, pr_s, pr_r, a_s, a_r, b_s, b_r,
):
    me = lax.axis_index("ctx")
    head = lax.axis_index("head")
    x = head // 2
    core = head % 2
    g = x
    odd = g % 2
    n = N_CTX
    sib = {"head": x * 2 + 1 - core}
    up = {"head": ((x + 1) % 4) * 2 + core}
    down = {"head": ((x + 3) % 4) * 2 + core}

    def remote(src, dst, ss, rs, dev):
        return pltpu.make_async_remote_copy(src, dst, ss, rs, device_id=dev, device_id_type=MESH)

    bar = pltpu.get_barrier_semaphore()
    each(1, n, lambda i: pl.semaphore_signal(bar, inc=1, device_id={"ctx": (me + i) % n}, device_id_type=MESH))
    for dev in (sib, up, down):
        pl.semaphore_signal(bar, inc=1, device_id=dev, device_id_type=MESH)

    loads = [
        pltpu.make_async_copy(picks_hbm, picks, lsem.at[0]),
        pltpu.make_async_copy(key_hbm.at[:, pl.ds(pl.multiple_of((g // 2) * 384, 128), 384)], kbuf, lsem.at[1]),
        pltpu.make_async_copy(val_hbm.at[:, pl.ds(pl.multiple_of(g * DV, 128), DV)], vbuf, lsem.at[2]),
        pltpu.make_async_copy(kw_hbm.at[:, pl.ds(pl.multiple_of((g // 2) * 384, 128), 384)], kw, lsem.at[3]),
        pltpu.make_async_copy(vw_hbm.at[:, pl.ds(pl.multiple_of(g * DV, 128), DV)], vw, lsem.at[4]),
        pltpu.make_async_copy(gate_hbm, gate, lsem.at[5]),
        pltpu.make_async_copy(q_hbm, q, lsem.at[6]),
        pltpu.make_async_copy(w_hbm, w, lsem.at[7]),
    ]
    for c in loads:
        c.start()

    loads[0].wait()
    req, slot, dead = plan(picks[:, g, :], me)
    reqb[...] = jnp.broadcast_to(req, (8, 128))
    slotb[...] = jnp.broadcast_to(slot, (8, 128))
    to_s = pltpu.make_async_copy(slotb, slots, lsem.at[8])
    to_s.start()
    pl.semaphore_wait(bar, n - 1 + 3)

    def rq(o):
        return remote(reqb, reqin.at[me], rq_s.at[o], rq_r.at[me], {"ctx": o})

    def rq_in(t):
        return remote(reqb, reqin.at[t], rq_s.at[t], rq_r.at[t], {"ctx": t})

    each(0, me, lambda o: rq(o).start())

    ei = iota((128, 1024), 0)
    ej = iota((128, 1024), 1)
    d8 = jnp.broadcast_to(dead, (8, 128))
    for qb in range(4):
        m = jnp.dot(d8, one(ei == qb * 16 + (ej >> 6)), preferred_element_type=F32)
        rowb[qb] = jnp.where(m > 0.5, DEAD, 0.0)

    for c in loads[1:5]:
        c.wait()
    lane = iota((KBLK, 256), 1)
    oddv = (lane >= 0) & (lane * 0 + odd > 0)
    keep = (lane >= odd * 64) & (lane < QK + odd * 64)
    vx[:, DV:] = jnp.ones((vx.shape[0], DV), BF)
    cx[:, DV:] = jnp.ones((cx.shape[0], DV), BF)
    sx[:, DV:] = jnp.ones((sx.shape[0], DV), BF)

    def spread(block, start, n, even_ref, odd_ref, v_ref):
        r0 = pl.ds(pl.multiple_of(start, 16), n)
        r1 = pl.ds(pl.multiple_of(start + n, 16), n)
        wide = iota((n, 256), 1)
        y = jnp.where(wide < QK, block[:, 0:256].astype(F32), 0.0)
        even_ref[r0, :] = y.astype(BF)
        odd_ref[r0, :] = pltpu.roll(y, 64, 1).astype(BF)
        y = jnp.where(wide >= 64, block[:, 128:384].astype(F32), 0.0)
        odd_ref[r1, :] = y.astype(BF)
        even_ref[r1, :] = pltpu.roll(y, 192, 1).astype(BF)
        v_ref[r0, :DV] = block[:, 384:512]
        v_ref[r1, :DV] = block[:, 512:640]

    def fold(even, odd_half, v0, v1):
        return jnp.concatenate(
            [even[:, :128], even[:, 128:] + odd_half[:, :128], odd_half[:, 128:], v0, v1], axis=1
        )

    def pack(i):
        r = pl.ds(pl.multiple_of(i * KBLK, KBLK), KBLK)
        y = jnp.where(oddv, kbuf[r, 128:384].astype(F32), kbuf[r, 0:256].astype(F32))
        y = jnp.where(keep, y, 0.0)
        turned = pltpu.roll(y, 64, 1)
        back = pltpu.roll(y, 192, 1)
        even = jnp.where(oddv, back, y).astype(BF)
        odd_form = jnp.where(oddv, y, turned).astype(BF)
        v = vbuf[r, :]
        r2 = pl.ds(pl.multiple_of(WINDOW + i * KBLK, KBLK), KBLK)
        ke[r2, :] = even
        ko[r2, :] = odd_form
        vx[r2, :DV] = v
        pk[i] = fold(even[:32], odd_form[32:], v[:32], v[32:])

    for i in range(16):
        pack(i)
    rim_c = remote(
        pk.at[pl.ds(8 + 4 * core, 4)], rim.at[pl.ds(4 * core, 4)], rim_s.at[0], rim_r.at[0], {"ctx": (me + 1) % n}
    )
    rim_f = remote(rim.at[pl.ds(4 * core, 4)], rim.at[pl.ds(4 * core, 4)], rim_s.at[1], rim_r.at[1], sib)

    wk = jnp.where(oddv[:CBLK], kw[:, 128:384], kw[:, 0:256])
    wk = jnp.where(oddv[:CBLK], pltpu.roll(wk, 192, 1), wk)
    wv = vw[...]
    for b in range(32):
        r = slice(WINDOW + b * CBLK, WINDOW + (b + 1) * CBLK)
        crow[b : b + 1, :256] = jnp.sum(ke[r, :].astype(F32) * wk, axis=0, keepdims=True)
        crow[b : b + 1, 256:] = jnp.sum(vx[r, :DV].astype(F32) * wv, axis=0, keepdims=True)
    c0 = crow[:16]
    c1 = crow[16:]
    cown[...] = fold(c0[:, :256], pltpu.roll(c1[:, :256], 64, 1), c0[:, 256:], c1[:, 256:]).astype(BF)

    def cp(t):
        return remote(cown, comp.at[t - me], cp_s.at[t - me], cp_r.at[t - me], {"ctx": t})

    def cp_in(d):
        return remote(cown, comp.at[d], cp_s.at[d], cp_r.at[d], {"ctx": (me + d) % n})

    each(me + 1, n, lambda t: cp(t).start())

    @pl.when(me < n - 1)
    def _():
        rim_c.start()

    def sm(t):
        return pltpu.make_async_copy(reqin.at[t], reqs.at[t], sm_s.at[t])

    def take(t):
        rq_in(t).wait_recv()
        sm(t).start()

    each(me + 1, n, take)

    def bk(t):
        return remote(send.at[t], blk.at[pl.ds(me * 4 + 2 * core, 2)], bk_s.at[t], bk_r.at[me], {"ctx": t})

    def bk_in(o):
        return remote(send.at[o], blk.at[pl.ds(o * 4 + 2 * core, 2)], bk_s.at[o], bk_r.at[o], {"ctx": o})

    def fw(o):
        part = blk.at[pl.ds(o * 4 + 2 * core, 2)]
        return remote(part, part, fw_s.at[o], fw_r.at[o], sib)

    def fw_in(o):
        part = blk.at[pl.ds(o * 4 + 2 - 2 * core, 2)]
        return remote(part, part, fw_s.at[o], fw_r.at[o], sib)

    def give(t):
        sm(t).wait()
        for j in range(2):
            send[t, j] = pk[reqs[t, 0, me * 4 + 2 * core + j] & 15]
        bk(t).start()

    each(me + 1, n, give)

    def pass_on(o):
        bk_in(o).wait_recv()
        fw(o).start()

    loads[5].wait()
    for qb in range(4):
        sg = 1.0 / (1.0 + jnp.exp(-gate[:, qb * QBLK : (qb + 1) * QBLK]))
        gt[qb * QBLK : (qb + 1) * QBLK, :] = jnp.concatenate([sg, jnp.zeros((104, QBLK), F32)], axis=0).T
    for i in range(4):
        blk[me * 4 + i] = pk[4 * i]
    comp[0] = cown[...]

    def blank(d):
        comp[d] = jnp.zeros((16, 640), BF)

    each(me + 1, n, blank)

    @pl.when(me == 0)
    def _():
        rim[...] = jnp.zeros_like(rim)

    loads[6].wait()
    rows = iota((QBLK, QBLK), 0)
    cols = iota((QBLK, QBLK), 1)

    def window(qb):
        base = pl.multiple_of(qb * QBLK, QBLK)
        first = me * 1024 + base
        bw[:, :256] = jnp.where(cols >= rows, jnp.where(first < 512, DEAD, 0.0), DEAD)
        bw[:, 256:512] = jnp.full((QBLK, QBLK), jnp.where(first < 256, DEAD, 0.0))
        bw[:, 512:] = jnp.where(cols <= rows, 0.0, DEAD)
        r = pl.ds(base, QBLK)
        span = pl.ds(base, 768)
        for h in range(8):
            off = (h // 2) * 384 + (h % 2) * 128
            nw, dw = branch(q[r, off : off + 256], (ko if h % 2 else ke)[span, :], vx[span, :], bw[...])
            acc[r, h * DV : (h + 1) * DV] = (gt[r, 16 + h : 17 + h] / dw) * nw

    def compressed(qb):
        base = pl.multiple_of(qb * QBLK, QBLK)
        rowc = iota((QBLK, 512), 0)
        colc = iota((QBLK, 512), 1)
        bc[...] = jnp.where(
            colc < 32,
            jnp.where(colc * 32 + 31 <= base + rowc, 0.0, DEAD),
            jnp.where(colc < (me + 1) * 32, 0.0, DEAD),
        )
        r = pl.ds(base, QBLK)
        for h in range(8):
            off = (h // 2) * 384 + (h % 2) * 128
            nc, dc = branch(q[r, off : off + 256], (co if h % 2 else ce)[...], cx[...], bc[...])
            accc[r, h * DV : (h + 1) * DV] = (gt[r, h : h + 1] / jnp.maximum(dc, 1.0)) * nc

    def far_setup(qb):
        for j in range(PICKS):
            spread(blk[slots[0, qb * PICKS + j] & 63], j * KBLK, 32, se, so, sx)
        rs = iota((QBLK, 1024), 0)
        cs = iota((QBLK, 1024), 1)
        bs[...] = jnp.where((cs < 64) & (cs > rs), DEAD, jnp.broadcast_to(rowb[qb][0:1, :], (QBLK, 1024)))

    def far(qb):
        base = pl.multiple_of(qb * QBLK, QBLK)
        r = pl.ds(base, QBLK)
        top = pl.ds(pl.multiple_of(core * 128, 128), 128)
        low = pl.ds(pl.multiple_of(128 - core * 128, 128), 128)
        for h in range(8):
            off = (h // 2) * 384 + (h % 2) * 128
            ns, ds = branch(q[r, off : off + 256], (so if h % 2 else se)[...], sx[...], bs[...])
            c = slice(h * DV, (h + 1) * DV)
            y = (acc[r, c] + accc[r, c] + (gt[r, 8 + h : 9 + h] / ds) * ns).astype(BF)
            att[top, c] = y[:128]
            att[low, c] = y[128:]

    def pr(r, c):
        return remote(psend.at[r, c], precv.at[r, c], pr_s.at[r, c], pr_r.at[r, c], sib)

    def project(r):
        def side(i):
            c = jnp.where(r == 1, 1 - i, i)
            y = jnp.dot(att[...], w[:, pl.ds(pl.multiple_of(c * HALF, 128), HALF)], preferred_element_type=F32)
            psend[r, c] = y[128:].astype(BF)
            pr(r, c).start()
            mine[r, c] = y[:128]

        each(0, 2, side)

    A, B = 0, 1

    def total(r, c):
        pr(r, c).wait_recv()
        return mine[r, c] + precv[r, c].astype(F32)

    def hop_a(k):
        return remote(sa.at[k], ra.at[k], a_s.at[k], a_r.at[k], up)

    def hop_b(k):
        return remote(sb.at[k], rb.at[k], b_s.at[k], b_r.at[k], down)

    def block_of(r):
        return (x + jnp.where(r == 0, 2, jnp.where(r == 1, 1, jnp.where(r == 2, 3, 0)))) % 4

    def late(k):
        return jnp.where(x >= 3 - k, 2 - k, 3 - k)

    def ship0():
        sa[0] = total(0, A).astype(BF)
        hop_a(0).start()
        sb[0] = total(0, B).astype(BF)
        hop_b(0).start()

    def ship1():
        sa[1] = total(1, B).astype(BF)
        hop_a(1).start()
        own = total(1, A)
        hop_a(0).wait_recv()
        sa[2] = (own + ra[0].astype(F32)).astype(BF)
        hop_a(2).start()

    def ship2():
        sb[1] = total(2, A).astype(BF)
        hop_b(1).start()
        own = total(2, B)
        hop_b(0).wait_recv()
        sb[2] = (own + rb[0].astype(F32)).astype(BF)
        hop_b(2).start()

    third = me // 3

    def go(i):
        is_w = (i <= 2) | (i == 9)
        is_c = ((i >= 3) & (i <= 5)) | (i == 10)
        is_f = ((i >= 6) & (i <= 8)) | (i == 11)
        w_block = jnp.where(i == 9, x, late(i))
        c_block = jnp.where(i == 10, x, late(i - 3))
        r = jnp.where(i == 11, 3, i - 6)

        @pl.when(i == 3)
        def _():
            each(1, me + 1, lambda d: cp_in(d).wait_recv())
            for k in range(16):
                spread(comp[k], k * CBLK, 16, ce, co, cx)

        @pl.when(i == jnp.where(x >= 2, 1, 2))
        def _():
            @pl.when(me > 0)
            def _():
                rim_c.wait_recv()
                rim_f.start()

            @pl.when(me > 0)
            def _():
                rim_f.wait_recv()

            for j in range(8):
                spread(rim[j], j * KBLK, 32, ke, ko, vx)

        @pl.when(i == 4)
        def _():
            each(2 * third, me, pass_on)

        @pl.when(i == 5)
        def _():
            each(third, 2 * third, pass_on)

        @pl.when(i == 6)
        def _():
            each(0, third, pass_on)
            loads[7].wait()
            to_s.wait()
            each(0, me, lambda o: fw_in(o).wait_recv())

        @pl.when(is_w)
        def _():
            window(w_block)

        @pl.when(is_c)
        def _():
            compressed(c_block)

        @pl.when(is_f)
        def _():
            far_setup(block_of(r))

            @pl.when(i == 7)
            def _():
                ship0()

            @pl.when(i == 8)
            def _():
                ship1()

            far(block_of(r))
            project(r)

        @pl.when(i == 8)
        def _():
            ship2()

    each(0, 12, go)
    own_a = total(3, A)
    hop_a(2).wait_recv()
    hop_b(1).wait_recv()
    outb[:, :HALF] = (own_a + ra[2].astype(F32) + rb[1].astype(F32)).astype(BF)
    own_b = total(3, B)
    hop_a(1).wait_recv()
    hop_b(2).wait_recv()
    outb[:, HALF:] = (own_b + ra[1].astype(F32) + rb[2].astype(F32)).astype(BF)
    done = pltpu.make_async_copy(outb, o_hbm, lsem.at[9])
    done.start()

    each(0, me, lambda o: rq(o).wait_send())
    each(me + 1, n, lambda t: cp(t).wait_send())
    each(me + 1, n, lambda t: bk(t).wait_send())
    each(0, me, lambda o: fw(o).wait_send())

    @pl.when(me < n - 1)
    def _():
        rim_c.wait_send()

    @pl.when(me > 0)
    def _():
        rim_f.wait_send()

    for r in range(4):
        pr(r, A).wait_send()
        pr(r, B).wait_send()
    for k in range(3):
        hop_a(k).wait_send()
        hop_b(k).wait_send()
    done.wait()


def local(queries, key_rows, value_rows, kw, vw, picks, gate, w):
    hbm = pl.BlockSpec(memory_space=pl.ANY)
    V = pltpu.VMEM
    D = pltpu.SemaphoreType.DMA
    return pl.pallas_call(
        layer,
        in_specs=[hbm] * 8,
        out_specs=hbm,
        out_shape=jax.ShapeDtypeStruct((128, 2560), BF),
        scratch_shapes=[
            V((1024, 1536), BF), V((1024, 384), BF), V((1024, DV), BF), V((CBLK, 384), F32), V((CBLK, DV), F32),
            V((4, 4, PICKS), I32), V((24, 1024), F32), V((1024, 2560), BF), V((1024, 128), F32),
            V((16, 32, 640), BF), V((32, 384), F32), V((16, 640), BF), V((8, 128), I32), V((16, 8, 128), I32),
            pltpu.SMEM((16, 8, 128), I32), V((8, 128), I32), pltpu.SMEM((8, 128), I32),
            V((16, 2, 32, 640), BF), V((64, 32, 640), BF), V((16, 16, 640), BF), V((8, 32, 640), BF),
            V((1536, 256), BF), V((1536, 256), BF), V((1536, 256), BF),
            V((512, 256), BF), V((512, 256), BF), V((512, 256), BF),
            V((1024, 256), BF), V((1024, 256), BF), V((1024, 256), BF),
            V((QBLK, 768), F32), V((QBLK, 512), F32), V((QBLK, 1024), F32), V((4, 8, 1024), F32),
            V((1024, 1024), F32), V((1024, 1024), F32), V((QBLK, 1024), BF),
            V((4, 2, 128, HALF), F32), V((4, 2, 128, HALF), BF), V((4, 2, 128, HALF), BF),
            V((3, 128, HALF), BF), V((3, 128, HALF), BF), V((3, 128, HALF), BF), V((3, 128, HALF), BF),
            V((128, 2560), BF),
            D((10,)), D((16,)), D((16,)), D((16,)), D((2,)), D((2,)), D((16,)), D((16,)), D((16,)), D((16,)), D((16,)), D((16,)),
            D((4, 2)), D((4, 2)), D((3,)), D((3,)), D((3,)), D((3,)),
        ],
        compiler_params=pltpu.CompilerParams(
            collective_id=0, has_side_effects=True, vmem_limit_bytes=60 << 20
        ),
    )(queries, key_rows, value_rows, kw, vw, picks, gate.transpose(1, 2, 0).reshape(24, 1024), w)


def solution(mesh):
    placed = (
        P("ctx", "head"), P("ctx", None), P("ctx", None), P(), P(),
        P("ctx", None, None), P("ctx", None, "head"), P("head", None),
    )
    return jax.shard_map(
        local, mesh=mesh, in_specs=placed, out_specs=P(("ctx", "head"), None), check_vma=False
    )
```

```python
import math

import jax
import jax.numpy as jnp
from jax import lax
from jax.experimental import pallas as pl
from jax.experimental.pallas import tpu as pltpu
from jax.sharding import PartitionSpec as P

QK = 192
DV = 128
CBLK = 32
KBLK = 64
PICKS = 16
WINDOW = 512
QBLK = 256
N_CTX = 16
DEAD = -1e30
FLOOR = -1e20
SCALE2 = QK**-0.5 * math.log2(math.e)
BF = jnp.bfloat16
F32 = jnp.float32
I32 = jnp.int32
MESH = pl.DeviceIdType.MESH
HALF = 1280


def one(x):
    return jnp.where(x, 1.0, 0.0)


def iota(shape, axis):
    return lax.broadcasted_iota(I32, shape, axis)


def plan(picks, shard):
    pos = iota((4, PICKS), 1)
    own = shard * 16 + 4 * iota((4, PICKS), 0)
    at = jnp.min(jnp.where(picks == own, pos, PICKS), axis=1, keepdims=True)
    p = jnp.where(pos == 0, own, jnp.where(pos == at, picks[:, 0:1], picks))
    row = jnp.concatenate([p[i : i + 1] for i in range(4)] + [jnp.full((1, 64), -1, I32)], axis=1)
    pr = jnp.broadcast_to(row, (128, 128))
    pc = pr.astype(F32).T.astype(I32)
    ri = iota((128, 128), 0)
    ci = iota((128, 128), 1)
    same = pr == pc
    dup = jnp.sum(one(same & (ri < ci) & ((ri >> 4) == (ci >> 4))), axis=0, keepdims=True)
    new_r = one((jnp.sum(one(same & (ri < ci)), axis=0, keepdims=True) == 0) & (ci[:1] < 64))
    new_c = one((jnp.sum(one(same & (ci < ri)), axis=1, keepdims=True) == 0) & (ri[:, :1] < 64))
    mates = (pr >> 4) == (pc >> 4)
    rank_r = jnp.sum(jnp.where(mates & (pc < pr), new_c, 0.0), axis=0, keepdims=True).astype(I32)
    rank_c = jnp.sum(jnp.where(mates & (pr < pc), new_r, 0.0), axis=1, keepdims=True).astype(I32)
    slot_r = (row >> 4) * 4 + rank_r
    slot_c = (pc[:, :1] >> 4) * 4 + rank_c
    req = jnp.sum(jnp.where(slot_c == ci, new_c, 0.0) * (pc & 15).astype(F32), axis=0, keepdims=True)
    dead = one((dup > 0) | (row > shard * 16 + 4 * (ci[:1] >> 4)) | (ci[:1] >= 64))
    return req.astype(I32), slot_r, dead


def branch(q, k, v, bias):
    s = lax.dot_general(q, k, (((1,), (1,)), ((), ())), preferred_element_type=F32) + bias
    top = jnp.maximum(jnp.max(s, axis=1, keepdims=True), FLOOR)
    w = jnp.exp2((s - top) * SCALE2).astype(BF)
    acc = jnp.dot(w, v, preferred_element_type=F32)
    return acc[:, :DV], acc[:, DV:]


def named_branch(q, k, v, tri, row):
    s = lax.dot_general(q, k, (((1,), (1,)), ((), ())), preferred_element_type=F32)
    s = jnp.concatenate([s[:, :128] + tri, s[:, 128:] + row], axis=1)
    top = jnp.maximum(jnp.max(s, axis=1, keepdims=True), FLOOR)
    w = jnp.exp2((s - top) * SCALE2).astype(BF)
    acc = jnp.dot(w, v, preferred_element_type=F32)
    return acc[:, :DV], acc[:, DV:]


def each(lo, hi, act):
    def step(i, carry):
        act(i)
        return carry

    lax.fori_loop(lo, hi, step, 0)


def layer(
    q_hbm, key_hbm, val_hbm, kw_hbm, vw_hbm, picks_hbm, gate_hbm, w_hbm, o_hbm,
    q, kbuf, vbuf, kw, vw, picks, gate, w, gt,
    pk, crow, cown, reqb, reqin, reqs, slotb, slots, send, blk, comp, rim,
    ke, ko, vx, ce, co, cx, se, so, sx, bw, bc, bs, rowb, acc, accc, att,
    mine, psend, precv, sa, ra, sb, rb, outb,
    lsem, sm_s, rq_s, rq_r, rim_s, rim_r, cp_s, cp_r, bk_s, bk_r, fw_s, fw_r, pr_s, pr_r, a_s, a_r, b_s, b_r,
):
    me = lax.axis_index("ctx")
    head = lax.axis_index("head")
    x = head // 2
    core = head % 2
    g = x
    odd = g % 2
    n = N_CTX
    sib = {"head": x * 2 + 1 - core}
    up = {"head": ((x + 1) % 4) * 2 + core}
    down = {"head": ((x + 3) % 4) * 2 + core}

    def remote(src, dst, ss, rs, dev):
        return pltpu.make_async_remote_copy(src, dst, ss, rs, device_id=dev, device_id_type=MESH)

    bar = pltpu.get_barrier_semaphore()
    each(1, n, lambda i: pl.semaphore_signal(bar, inc=1, device_id={"ctx": (me + i) % n}, device_id_type=MESH))
    for dev in (sib, up, down):
        pl.semaphore_signal(bar, inc=1, device_id=dev, device_id_type=MESH)

    loads = [
        pltpu.make_async_copy(picks_hbm, picks, lsem.at[0]),
        pltpu.make_async_copy(key_hbm.at[:, pl.ds(pl.multiple_of((g // 2) * 384, 128), 384)], kbuf, lsem.at[1]),
        pltpu.make_async_copy(val_hbm.at[:, pl.ds(pl.multiple_of(g * DV, 128), DV)], vbuf, lsem.at[2]),
        pltpu.make_async_copy(kw_hbm.at[:, pl.ds(pl.multiple_of((g // 2) * 384, 128), 384)], kw, lsem.at[3]),
        pltpu.make_async_copy(vw_hbm.at[:, pl.ds(pl.multiple_of(g * DV, 128), DV)], vw, lsem.at[4]),
        pltpu.make_async_copy(gate_hbm, gate, lsem.at[5]),
        pltpu.make_async_copy(q_hbm, q, lsem.at[6]),
        pltpu.make_async_copy(w_hbm, w, lsem.at[7]),
    ]
    for c in loads:
        c.start()

    loads[0].wait()
    req, slot, dead = plan(picks[:, g, :], me)
    reqb[...] = jnp.broadcast_to(req, (8, 128))
    slotb[...] = jnp.broadcast_to(slot, (8, 128))
    to_s = pltpu.make_async_copy(slotb, slots, lsem.at[8])
    to_s.start()
    pl.semaphore_wait(bar, n - 1 + 3)

    def rq(o):
        return remote(reqb, reqin.at[me], rq_s.at[o], rq_r.at[me], {"ctx": o})

    def rq_in(t):
        return remote(reqb, reqin.at[t], rq_s.at[t], rq_r.at[t], {"ctx": t})

    each(0, me, lambda o: rq(o).start())

    ei = iota((128, 1024), 0)
    ej = iota((128, 1024), 1)
    d8 = jnp.broadcast_to(dead, (8, 128))
    for qb in range(4):
        m = jnp.dot(d8, one(ei == qb * 16 + (ej >> 6)), preferred_element_type=F32)
        rowb[qb] = jnp.where(m > 0.5, DEAD, 0.0)

    for c in loads[1:5]:
        c.wait()
    lane = iota((KBLK, 256), 1)
    oddv = (lane >= 0) & (lane * 0 + odd > 0)
    keep = (lane >= odd * 64) & (lane < QK + odd * 64)
    vx[:, DV:] = jnp.ones((vx.shape[0], DV), BF)
    cx[:, DV:] = jnp.ones((cx.shape[0], DV), BF)
    sx[:, DV:] = jnp.ones((sx.shape[0], DV), BF)

    def spread(block, start, n, even_ref, odd_ref, v_ref):
        r0 = pl.ds(pl.multiple_of(start, 16), n)
        r1 = pl.ds(pl.multiple_of(start + n, 16), n)
        wide = iota((n, 256), 1)
        y = jnp.where(wide < QK, block[:, 0:256].astype(F32), 0.0)
        even_ref[r0, :] = y.astype(BF)
        odd_ref[r0, :] = pltpu.roll(y, 64, 1).astype(BF)
        y = jnp.where(wide >= 64, block[:, 128:384].astype(F32), 0.0)
        odd_ref[r1, :] = y.astype(BF)
        even_ref[r1, :] = pltpu.roll(y, 192, 1).astype(BF)
        v_ref[r0, :DV] = block[:, 384:512]
        v_ref[r1, :DV] = block[:, 512:640]

    def fold(even, odd_half, v0, v1):
        return jnp.concatenate(
            [even[:, :128], even[:, 128:] + odd_half[:, :128], odd_half[:, 128:], v0, v1], axis=1
        )

    def pack(i):
        r = pl.ds(pl.multiple_of(i * KBLK, KBLK), KBLK)
        y = jnp.where(oddv, kbuf[r, 128:384].astype(F32), kbuf[r, 0:256].astype(F32))
        y = jnp.where(keep, y, 0.0)
        turned = pltpu.roll(y, 64, 1)
        back = pltpu.roll(y, 192, 1)
        even = jnp.where(oddv, back, y).astype(BF)
        odd_form = jnp.where(oddv, y, turned).astype(BF)
        v = vbuf[r, :]
        r2 = pl.ds(pl.multiple_of(WINDOW + i * KBLK, KBLK), KBLK)
        ke[r2, :] = even
        ko[r2, :] = odd_form
        vx[r2, :DV] = v
        pk[i] = fold(even[:32], odd_form[32:], v[:32], v[32:])

    for i in range(16):
        pack(i)
    rim_c = remote(
        pk.at[pl.ds(8 + 4 * core, 4)], rim.at[pl.ds(4 * core, 4)], rim_s.at[0], rim_r.at[0], {"ctx": (me + 1) % n}
    )
    rim_f = remote(rim.at[pl.ds(4 * core, 4)], rim.at[pl.ds(4 * core, 4)], rim_s.at[1], rim_r.at[1], sib)

    @pl.when(me < n - 1)
    def _():
        rim_c.start()

    wk = jnp.where(oddv[:CBLK], kw[:, 128:384], kw[:, 0:256])
    wk = jnp.where(oddv[:CBLK], pltpu.roll(wk, 192, 1), wk)
    wv = vw[...]
    for b in range(32):
        r = slice(WINDOW + b * CBLK, WINDOW + (b + 1) * CBLK)
        crow[b : b + 1, :256] = jnp.sum(ke[r, :].astype(F32) * wk, axis=0, keepdims=True)
        crow[b : b + 1, 256:] = jnp.sum(vx[r, :DV].astype(F32) * wv, axis=0, keepdims=True)
    c0 = crow[:16]
    c1 = crow[16:]
    cown[...] = fold(c0[:, :256], pltpu.roll(c1[:, :256], 64, 1), c0[:, 256:], c1[:, 256:]).astype(BF)

    def cp(t):
        return remote(cown, comp.at[t - me], cp_s.at[t - me], cp_r.at[t - me], {"ctx": t})

    def cp_in(d):
        return remote(cown, comp.at[d], cp_s.at[d], cp_r.at[d], {"ctx": (me + d) % n})

    each(me + 1, n, lambda t: cp(t).start())

    def sm(t):
        return pltpu.make_async_copy(reqin.at[t], reqs.at[t], sm_s.at[t])

    def take(t):
        rq_in(t).wait_recv()
        sm(t).start()


    def bk(t):
        return remote(send.at[t], blk.at[pl.ds(me * 4 + 2 * core, 2)], bk_s.at[t], bk_r.at[me], {"ctx": t})

    def bk_in(o):
        return remote(send.at[o], blk.at[pl.ds(o * 4 + 2 * core, 2)], bk_s.at[o], bk_r.at[o], {"ctx": o})

    def fw(o):
        part = blk.at[pl.ds(o * 4 + 2 * core, 2)]
        return remote(part, part, fw_s.at[o], fw_r.at[o], sib)

    def fw_in(o):
        part = blk.at[pl.ds(o * 4 + 2 - 2 * core, 2)]
        return remote(part, part, fw_s.at[o], fw_r.at[o], sib)

    def give(t):
        sm(t).wait()
        for j in range(2):
            send[t, j] = pk[reqs[t, 0, me * 4 + 2 * core + j] & 15]
        bk(t).start()


    def pass_on(o):
        bk_in(o).wait_recv()
        fw(o).start()

    loads[5].wait()
    for qb in range(4):
        sg = 1.0 / (1.0 + jnp.exp(-gate[:, qb * QBLK : (qb + 1) * QBLK]))
        gt[qb * QBLK : (qb + 1) * QBLK, :] = jnp.concatenate([sg, jnp.zeros((104, QBLK), F32)], axis=0).T
    for i in range(4):
        blk[me * 4 + i] = pk[4 * i]
    comp[0] = cown[...]

    def blank(d):
        comp[d] = jnp.zeros((16, 640), BF)

    each(me + 1, n, blank)

    @pl.when(me == 0)
    def _():
        rim[...] = jnp.zeros_like(rim)

    loads[6].wait()
    rows = iota((QBLK, QBLK), 0)
    cols = iota((QBLK, QBLK), 1)

    def window(qb):
        base = pl.multiple_of(qb * QBLK, QBLK)
        first = me * 1024 + base
        bw[:, :256] = jnp.where(cols >= rows, jnp.where(first < 512, DEAD, 0.0), DEAD)
        bw[:, 256:512] = jnp.full((QBLK, QBLK), jnp.where(first < 256, DEAD, 0.0))
        bw[:, 512:] = jnp.where(cols <= rows, 0.0, DEAD)
        r = pl.ds(base, QBLK)
        span = pl.ds(base, 768)
        for h in range(8):
            off = (h // 2) * 384 + (h % 2) * 128
            nw, dw = branch(q[r, off : off + 256], (ko if h % 2 else ke)[span, :], vx[span, :], bw[...])
            acc[r, h * DV : (h + 1) * DV] = (gt[r, 16 + h : 17 + h] / dw) * nw

    def compressed(qb):
        base = pl.multiple_of(qb * QBLK, QBLK)
        rowc = iota((QBLK, 512), 0)
        colc = iota((QBLK, 512), 1)
        bc[...] = jnp.where(
            colc < 32,
            jnp.where(colc * 32 + 31 <= base + rowc, 0.0, DEAD),
            jnp.where(colc < (me + 1) * 32, 0.0, DEAD),
        )
        r = pl.ds(base, QBLK)
        for h in range(8):
            off = (h // 2) * 384 + (h % 2) * 128
            nc, dc = branch(q[r, off : off + 256], (co if h % 2 else ce)[...], cx[...], bc[...])
            accc[r, h * DV : (h + 1) * DV] = (gt[r, h : h + 1] / jnp.maximum(dc, 1.0)) * nc

    def far_setup(qb):
        for j in range(PICKS):
            spread(blk[slots[0, qb * PICKS + j] & 63], j * KBLK, 32, se, so, sx)
        rs = iota((QBLK, 128), 0)
        cs = iota((QBLK, 128), 1)
        bs[...] = jnp.where((cs < 64) & (cs > rs), DEAD, jnp.broadcast_to(rowb[qb][0:1, :128], (QBLK, 128)))

    def far(qb):
        base = pl.multiple_of(qb * QBLK, QBLK)
        r = pl.ds(base, QBLK)
        top = pl.ds(pl.multiple_of(core * 128, 128), 128)
        low = pl.ds(pl.multiple_of(128 - core * 128, 128), 128)
        for h in range(8):
            off = (h // 2) * 384 + (h % 2) * 128
            ns, ds = named_branch(
                q[r, off : off + 256], (so if h % 2 else se)[...], sx[...], bs[...], rowb[qb][0:1, 128:]
            )
            c = slice(h * DV, (h + 1) * DV)
            y = (acc[r, c] + accc[r, c] + (gt[r, 8 + h : 9 + h] / ds) * ns).astype(BF)
            att[top, c] = y[:128]
            att[low, c] = y[128:]

    def pr(r, c):
        return remote(psend.at[r, c], precv.at[r, c], pr_s.at[r, c], pr_r.at[r, c], sib)

    def project(r):
        def side(i):
            c = jnp.where(r == 1, 1 - i, i)
            y = jnp.dot(att[...], w[:, pl.ds(pl.multiple_of(c * HALF, 128), HALF)], preferred_element_type=F32)
            psend[r, c] = y[128:].astype(BF)
            pr(r, c).start()
            mine[r, c] = y[:128]

        each(0, 2, side)

    A, B = 0, 1

    def total(r, c):
        pr(r, c).wait_recv()
        return mine[r, c] + precv[r, c].astype(F32)

    def hop_a(k):
        return remote(sa.at[k], ra.at[k], a_s.at[k], a_r.at[k], up)

    def hop_b(k):
        return remote(sb.at[k], rb.at[k], b_s.at[k], b_r.at[k], down)

    def block_of(r):
        return (x + jnp.where(r == 0, 2, jnp.where(r == 1, 1, jnp.where(r == 2, 3, 0)))) % 4

    def late(k):
        return jnp.where(x >= 3 - k, 2 - k, 3 - k)

    def ship0():
        sa[0] = total(0, A).astype(BF)
        hop_a(0).start()
        sb[0] = total(0, B).astype(BF)
        hop_b(0).start()

    def ship1():
        sa[1] = total(1, B).astype(BF)
        hop_a(1).start()
        own = total(1, A)
        hop_a(0).wait_recv()
        sa[2] = (own + ra[0].astype(F32)).astype(BF)
        hop_a(2).start()

    def ship2():
        sb[1] = total(2, A).astype(BF)
        hop_b(1).start()

    def ship3():
        own = total(2, B)
        hop_b(0).wait_recv()
        sb[2] = (own + rb[0].astype(F32)).astype(BF)
        hop_b(2).start()

    third = me // 3
    early = (me % 4 == 0) & (me > 0) & (x >= 2)

    def go(i):
        is_w = (i <= 2) | ((i == 3) & early) | ((i == 10) & jnp.logical_not(early))
        is_c = ((i >= 4) & (i <= 6)) | (i == 11)
        is_f = ((i >= 7) & (i <= 9)) | (i == 12)
        w_block = jnp.where(
            (i == 10) | ((i == 1) & early), x, late(jnp.where(early & (i >= 2), i - 1, i))
        )
        c_block = jnp.where(i == 11, x, late(i - 4))
        r = jnp.where(i == 12, 3, i - 7)

        @pl.when(i == 4)
        def _():
            each(1, me + 1, lambda d: cp_in(d).wait_recv())
            for k in range(16):
                spread(comp[k], k * CBLK, 16, ce, co, cx)

        @pl.when(i == jnp.where((x >= 2) & jnp.logical_not(early), 1, 2))
        def _():
            @pl.when(me > 0)
            def _():
                rim_c.wait_recv()
                rim_f.start()

            @pl.when(me > 0)
            def _():
                rim_f.wait_recv()

            for j in range(8):
                spread(rim[j], j * KBLK, 32, ke, ko, vx)

        @pl.when(i == 5)
        def _():
            each(2 * third, me, pass_on)

        @pl.when(i == 6)
        def _():
            each(third, 2 * third, pass_on)

        @pl.when(i == 7)
        def _():
            each(0, third, pass_on)
            loads[7].wait()
            to_s.wait()
            each(0, me, lambda o: fw_in(o).wait_recv())

        @pl.when(is_w)
        def _():
            window(w_block)

        @pl.when(i == 0)
        def _():
            each(me + 1, n, take)
            each(me + 1, n, give)

        @pl.when(is_c)
        def _():
            compressed(c_block)

        @pl.when(is_f)
        def _():
            far_setup(block_of(r))

            @pl.when(i == 8)
            def _():
                ship0()

            @pl.when(i == 9)
            def _():
                ship1()

            far(block_of(r))
            project(r)

        @pl.when(i == 9)
        def _():
            ship2()

        @pl.when(i == 10)
        def _():
            ship3()

    each(0, 13, go)
    own_a = total(3, A)
    hop_a(2).wait_recv()
    hop_b(1).wait_recv()
    outb[:, :HALF] = (own_a + ra[2].astype(F32) + rb[1].astype(F32)).astype(BF)
    own_b = total(3, B)
    hop_a(1).wait_recv()
    hop_b(2).wait_recv()
    outb[:, HALF:] = (own_b + ra[1].astype(F32) + rb[2].astype(F32)).astype(BF)
    done = pltpu.make_async_copy(outb, o_hbm, lsem.at[9])
    done.start()

    each(0, me, lambda o: rq(o).wait_send())
    each(me + 1, n, lambda t: cp(t).wait_send())
    each(me + 1, n, lambda t: bk(t).wait_send())
    each(0, me, lambda o: fw(o).wait_send())

    @pl.when(me < n - 1)
    def _():
        rim_c.wait_send()

    @pl.when(me > 0)
    def _():
        rim_f.wait_send()

    for r in range(4):
        pr(r, A).wait_send()
        pr(r, B).wait_send()
    for k in range(3):
        hop_a(k).wait_send()
        hop_b(k).wait_send()
    done.wait()


def local(queries, key_rows, value_rows, kw, vw, picks, gate, w):
    hbm = pl.BlockSpec(memory_space=pl.ANY)
    V = pltpu.VMEM
    D = pltpu.SemaphoreType.DMA
    return pl.pallas_call(
        layer,
        in_specs=[hbm] * 8,
        out_specs=hbm,
        out_shape=jax.ShapeDtypeStruct((128, 2560), BF),
        scratch_shapes=[
            V((1024, 1536), BF), V((1024, 384), BF), V((1024, DV), BF), V((CBLK, 384), F32), V((CBLK, DV), F32),
            V((4, 4, PICKS), I32), V((24, 1024), F32), V((1024, 2560), BF), V((1024, 128), F32),
            V((16, 32, 640), BF), V((32, 384), F32), V((16, 640), BF), V((8, 128), I32), V((16, 8, 128), I32),
            pltpu.SMEM((16, 8, 128), I32), V((8, 128), I32), pltpu.SMEM((8, 128), I32),
            V((16, 2, 32, 640), BF), V((64, 32, 640), BF), V((16, 16, 640), BF), V((8, 32, 640), BF),
            V((1536, 256), BF), V((1536, 256), BF), V((1536, 256), BF),
            V((512, 256), BF), V((512, 256), BF), V((512, 256), BF),
            V((1024, 256), BF), V((1024, 256), BF), V((1024, 256), BF),
            V((QBLK, 768), F32), V((QBLK, 512), F32), V((QBLK, 128), F32), V((4, 8, 1024), F32),
            V((1024, 1024), F32), V((1024, 1024), F32), V((QBLK, 1024), BF),
            V((4, 2, 128, HALF), F32), V((4, 2, 128, HALF), BF), V((4, 2, 128, HALF), BF),
            V((3, 128, HALF), BF), V((3, 128, HALF), BF), V((3, 128, HALF), BF), V((3, 128, HALF), BF),
            V((128, 2560), BF),
            D((10,)), D((16,)), D((16,)), D((16,)), D((2,)), D((2,)), D((16,)), D((16,)), D((16,)), D((16,)), D((16,)), D((16,)),
            D((4, 2)), D((4, 2)), D((3,)), D((3,)), D((3,)), D((3,)),
        ],
        compiler_params=pltpu.CompilerParams(
            collective_id=0, has_side_effects=True, vmem_limit_bytes=60 << 20
        ),
    )(queries, key_rows, value_rows, kw, vw, picks, gate.transpose(1, 2, 0).reshape(24, 1024), w)


def solution(mesh):
    placed = (
        P("ctx", "head"), P("ctx", None), P("ctx", None), P(), P(),
        P("ctx", None, None), P("ctx", None, "head"), P("head", None),
    )
    return jax.shard_map(
        local, mesh=mesh, in_specs=placed, out_specs=P(("ctx", "head"), None), check_vma=False
    )
```

```python
import math

import jax
import jax.numpy as jnp
from jax import lax
from jax.experimental import pallas as pl
from jax.experimental.pallas import tpu as pltpu
from jax.sharding import PartitionSpec as P

QK = 192
DV = 128
CBLK = 32
KBLK = 64
PICKS = 16
WINDOW = 512
QBLK = 256
N_CTX = 16
DEAD = -1e30
FLOOR = -1e20
SCALE2 = QK**-0.5 * math.log2(math.e)
BF = jnp.bfloat16
F32 = jnp.float32
I32 = jnp.int32
MESH = pl.DeviceIdType.MESH
HALF = 1280


def one(x):
    return jnp.where(x, 1.0, 0.0)


def iota(shape, axis):
    return lax.broadcasted_iota(I32, shape, axis)


def plan(picks, shard):
    pos = iota((4, PICKS), 1)
    own = shard * 16 + 4 * iota((4, PICKS), 0)
    at = jnp.min(jnp.where(picks == own, pos, PICKS), axis=1, keepdims=True)
    p = jnp.where(pos == 0, own, jnp.where(pos == at, picks[:, 0:1], picks))
    row = jnp.concatenate([p[i : i + 1] for i in range(4)] + [jnp.full((1, 64), -1, I32)], axis=1)
    pr = jnp.broadcast_to(row, (128, 128))
    pc = pr.astype(F32).T.astype(I32)
    ri = iota((128, 128), 0)
    ci = iota((128, 128), 1)
    same = pr == pc
    dup = jnp.sum(one(same & (ri < ci) & ((ri >> 4) == (ci >> 4))), axis=0, keepdims=True)
    new_r = one((jnp.sum(one(same & (ri < ci)), axis=0, keepdims=True) == 0) & (ci[:1] < 64))
    new_c = one((jnp.sum(one(same & (ci < ri)), axis=1, keepdims=True) == 0) & (ri[:, :1] < 64))
    mates = (pr >> 4) == (pc >> 4)
    rank_r = jnp.sum(jnp.where(mates & (pc < pr), new_c, 0.0), axis=0, keepdims=True).astype(I32)
    rank_c = jnp.sum(jnp.where(mates & (pr < pc), new_r, 0.0), axis=1, keepdims=True).astype(I32)
    slot_r = (row >> 4) * 4 + rank_r
    slot_c = (pc[:, :1] >> 4) * 4 + rank_c
    req = jnp.sum(jnp.where(slot_c == ci, new_c, 0.0) * (pc & 15).astype(F32), axis=0, keepdims=True)
    dead = one((dup > 0) | (row > shard * 16 + 4 * (ci[:1] >> 4)) | (ci[:1] >= 64))
    return req.astype(I32), slot_r, dead


def branch(q, k, v, bias):
    s = lax.dot_general(q, k, (((1,), (1,)), ((), ())), preferred_element_type=F32) + bias
    top = jnp.maximum(jnp.max(s, axis=1, keepdims=True), FLOOR)
    w = jnp.exp2((s - top) * SCALE2).astype(BF)
    acc = jnp.dot(w, v, preferred_element_type=F32)
    return acc[:, :DV], acc[:, DV:]


def named_branch(q, k, v, tri, row):
    s = lax.dot_general(q, k, (((1,), (1,)), ((), ())), preferred_element_type=F32)
    s = jnp.concatenate([s[:, :128] + tri, s[:, 128:] + row], axis=1)
    top = jnp.maximum(jnp.max(s, axis=1, keepdims=True), FLOOR)
    w = jnp.exp2((s - top) * SCALE2).astype(BF)
    acc = jnp.dot(w, v, preferred_element_type=F32)
    return acc[:, :DV], acc[:, DV:]


def each(lo, hi, act):
    def step(i, carry):
        act(i)
        return carry

    lax.fori_loop(lo, hi, step, 0)


def layer(
    q_hbm, key_hbm, val_hbm, kw_hbm, vw_hbm, picks_hbm, gate_hbm, w_hbm, o_hbm,
    q, kbuf, vbuf, kw, vw, picks, gate, w, gt,
    pk, crow, cown, reqb, reqin, reqs, slotb, slots, send, blk, comp, rim,
    ke, ko, vx, ce, co, cx, se, so, sx, bw, bc, bs, rowb, acc, accc, att,
    mine, psend, precv, sa, ra, sb, rb, outb,
    lsem, sm_s, rq_s, rq_r, rim_s, rim_r, cp_s, cp_r, bk_s, bk_r, fw_s, fw_r, pr_s, pr_r, a_s, a_r, b_s, b_r,
):
    me = lax.axis_index("ctx")
    head = lax.axis_index("head")
    x = head // 2
    core = head % 2
    g = x
    odd = g % 2
    n = N_CTX
    sib = {"head": x * 2 + 1 - core}
    up = {"head": ((x + 1) % 4) * 2 + core}
    down = {"head": ((x + 3) % 4) * 2 + core}

    def remote(src, dst, ss, rs, dev):
        return pltpu.make_async_remote_copy(src, dst, ss, rs, device_id=dev, device_id_type=MESH)

    bar = pltpu.get_barrier_semaphore()
    each(1, n, lambda i: pl.semaphore_signal(bar, inc=1, device_id={"ctx": (me + i) % n}, device_id_type=MESH))
    for dev in (sib, up, down):
        pl.semaphore_signal(bar, inc=1, device_id=dev, device_id_type=MESH)

    loads = [
        pltpu.make_async_copy(picks_hbm, picks, lsem.at[0]),
        pltpu.make_async_copy(key_hbm.at[:, pl.ds(pl.multiple_of((g // 2) * 384, 128), 384)], kbuf, lsem.at[1]),
        pltpu.make_async_copy(val_hbm.at[:, pl.ds(pl.multiple_of(g * DV, 128), DV)], vbuf, lsem.at[2]),
        pltpu.make_async_copy(kw_hbm.at[:, pl.ds(pl.multiple_of((g // 2) * 384, 128), 384)], kw, lsem.at[3]),
        pltpu.make_async_copy(vw_hbm.at[:, pl.ds(pl.multiple_of(g * DV, 128), DV)], vw, lsem.at[4]),
        pltpu.make_async_copy(gate_hbm, gate, lsem.at[5]),
        pltpu.make_async_copy(q_hbm, q, lsem.at[6]),
        pltpu.make_async_copy(w_hbm, w, lsem.at[7]),
    ]
    for c in loads:
        c.start()

    loads[0].wait()
    req, slot, dead = plan(picks[:, g, :], me)
    reqb[...] = jnp.broadcast_to(req, (8, 128))
    slotb[...] = jnp.broadcast_to(slot, (8, 128))
    to_s = pltpu.make_async_copy(slotb, slots, lsem.at[8])
    to_s.start()
    pl.semaphore_wait(bar, n - 1 + 3)

    def rq(o):
        return remote(reqb, reqin.at[me], rq_s.at[o], rq_r.at[me], {"ctx": o})

    def rq_in(t):
        return remote(reqb, reqin.at[t], rq_s.at[t], rq_r.at[t], {"ctx": t})

    each(0, me, lambda o: rq(o).start())

    ei = iota((128, 1024), 0)
    ej = iota((128, 1024), 1)
    d8 = jnp.broadcast_to(dead, (8, 128))
    for qb in range(4):
        m = jnp.dot(d8, one(ei == qb * 16 + (ej >> 6)), preferred_element_type=F32)
        rowb[qb] = jnp.where(m > 0.5, DEAD, 0.0)

    for c in loads[1:5]:
        c.wait()
    lane = iota((KBLK, 256), 1)
    oddv = (lane >= 0) & (lane * 0 + odd > 0)
    keep = (lane >= odd * 64) & (lane < QK + odd * 64)
    vx[:, DV:] = jnp.ones((vx.shape[0], DV), BF)
    cx[:, DV:] = jnp.ones((cx.shape[0], DV), BF)
    sx[:, DV:] = jnp.ones((sx.shape[0], DV), BF)

    def spread(block, start, n, even_ref, odd_ref, v_ref):
        r0 = pl.ds(pl.multiple_of(start, 16), n)
        r1 = pl.ds(pl.multiple_of(start + n, 16), n)
        wide = iota((n, 256), 1)
        y = jnp.where(wide < QK, block[:, 0:256].astype(F32), 0.0)
        even_ref[r0, :] = y.astype(BF)
        odd_ref[r0, :] = pltpu.roll(y, 64, 1).astype(BF)
        y = jnp.where(wide >= 64, block[:, 128:384].astype(F32), 0.0)
        odd_ref[r1, :] = y.astype(BF)
        even_ref[r1, :] = pltpu.roll(y, 192, 1).astype(BF)
        v_ref[r0, :DV] = block[:, 384:512]
        v_ref[r1, :DV] = block[:, 512:640]

    def fold(even, odd_half, v0, v1):
        return jnp.concatenate(
            [even[:, :128], even[:, 128:] + odd_half[:, :128], odd_half[:, 128:], v0, v1], axis=1
        )

    def pack(i):
        r = pl.ds(pl.multiple_of(i * KBLK, KBLK), KBLK)
        y = jnp.where(oddv, kbuf[r, 128:384].astype(F32), kbuf[r, 0:256].astype(F32))
        y = jnp.where(keep, y, 0.0)
        turned = pltpu.roll(y, 64, 1)
        back = pltpu.roll(y, 192, 1)
        even = jnp.where(oddv, back, y).astype(BF)
        odd_form = jnp.where(oddv, y, turned).astype(BF)
        v = vbuf[r, :]
        r2 = pl.ds(pl.multiple_of(WINDOW + i * KBLK, KBLK), KBLK)
        ke[r2, :] = even
        ko[r2, :] = odd_form
        vx[r2, :DV] = v
        pk[i] = fold(even[:32], odd_form[32:], v[:32], v[32:])

    for i in range(16):
        pack(i)
    rim_c = remote(
        pk.at[pl.ds(8 + 4 * core, 4)], rim.at[pl.ds(4 * core, 4)], rim_s.at[0], rim_r.at[0], {"ctx": (me + 1) % n}
    )
    rim_f = remote(rim.at[pl.ds(4 * core, 4)], rim.at[pl.ds(4 * core, 4)], rim_s.at[1], rim_r.at[1], sib)

    @pl.when(me < n - 1)
    def _():
        rim_c.start()

    wk = jnp.where(oddv[:CBLK], kw[:, 128:384], kw[:, 0:256])
    wk = jnp.where(oddv[:CBLK], pltpu.roll(wk, 192, 1), wk)
    wv = vw[...]
    for b in range(32):
        r = slice(WINDOW + b * CBLK, WINDOW + (b + 1) * CBLK)
        crow[b : b + 1, :256] = jnp.sum(ke[r, :].astype(F32) * wk, axis=0, keepdims=True)
        crow[b : b + 1, 256:] = jnp.sum(vx[r, :DV].astype(F32) * wv, axis=0, keepdims=True)
    c0 = crow[:16]
    c1 = crow[16:]
    cown[...] = fold(c0[:, :256], pltpu.roll(c1[:, :256], 64, 1), c0[:, 256:], c1[:, 256:]).astype(BF)

    def cp(t):
        return remote(cown, comp.at[t - me], cp_s.at[t - me], cp_r.at[t - me], {"ctx": t})

    def cp_in(d):
        return remote(cown, comp.at[d], cp_s.at[d], cp_r.at[d], {"ctx": (me + d) % n})

    each(me + 1, n, lambda t: cp(t).start())

    def sm(t):
        return pltpu.make_async_copy(reqin.at[t], reqs.at[t], sm_s.at[t])

    def take(t):
        rq_in(t).wait_recv()
        sm(t).start()


    def bk(t):
        return remote(send.at[t], blk.at[pl.ds(me * 4 + 2 * core, 2)], bk_s.at[t], bk_r.at[me], {"ctx": t})

    def bk_in(o):
        return remote(send.at[o], blk.at[pl.ds(o * 4 + 2 * core, 2)], bk_s.at[o], bk_r.at[o], {"ctx": o})

    def fw(o):
        part = blk.at[pl.ds(o * 4 + 2 * core, 2)]
        return remote(part, part, fw_s.at[o], fw_r.at[o], sib)

    def fw_in(o):
        part = blk.at[pl.ds(o * 4 + 2 - 2 * core, 2)]
        return remote(part, part, fw_s.at[o], fw_r.at[o], sib)

    def give(t):
        sm(t).wait()
        for j in range(2):
            send[t, j] = pk[reqs[t, 0, me * 4 + 2 * core + j] & 15]
        bk(t).start()


    def pass_on(o):
        bk_in(o).wait_recv()
        fw(o).start()

    loads[5].wait()
    for qb in range(4):
        sg = 1.0 / (1.0 + jnp.exp(-gate[:, qb * QBLK : (qb + 1) * QBLK]))
        gt[qb * QBLK : (qb + 1) * QBLK, :] = jnp.concatenate([sg, jnp.zeros((104, QBLK), F32)], axis=0).T
    for i in range(4):
        blk[me * 4 + i] = pk[4 * i]
    comp[0] = cown[...]

    def blank(d):
        comp[d] = jnp.zeros((16, 640), BF)

    each(me + 1, n, blank)

    @pl.when(me == 0)
    def _():
        rim[...] = jnp.zeros_like(rim)

    loads[6].wait()
    rows = iota((QBLK, QBLK), 0)
    cols = iota((QBLK, QBLK), 1)

    def window(qb):
        base = pl.multiple_of(qb * QBLK, QBLK)
        first = me * 1024 + base
        bw[:, :256] = jnp.where(cols >= rows, jnp.where(first < 512, DEAD, 0.0), DEAD)
        bw[:, 256:512] = jnp.full((QBLK, QBLK), jnp.where(first < 256, DEAD, 0.0))
        bw[:, 512:] = jnp.where(cols <= rows, 0.0, DEAD)
        r = pl.ds(base, QBLK)
        span = pl.ds(base, 768)
        for h in range(8):
            off = (h // 2) * 384 + (h % 2) * 128
            nw, dw = branch(q[r, off : off + 256], (ko if h % 2 else ke)[span, :], vx[span, :], bw[...])
            acc[r, h * DV : (h + 1) * DV] = (gt[r, 16 + h : 17 + h] / dw) * nw

    def compressed(qb):
        base = pl.multiple_of(qb * QBLK, QBLK)
        rowc = iota((QBLK, 512), 0)
        colc = iota((QBLK, 512), 1)
        bc[...] = jnp.where(
            colc < 32,
            jnp.where(colc * 32 + 31 <= base + rowc, 0.0, DEAD),
            jnp.where(colc < (me + 1) * 32, 0.0, DEAD),
        )
        r = pl.ds(base, QBLK)
        for h in range(8):
            off = (h // 2) * 384 + (h % 2) * 128
            nc, dc = branch(q[r, off : off + 256], (co if h % 2 else ce)[...], cx[...], bc[...])
            accc[r, h * DV : (h + 1) * DV] = (gt[r, h : h + 1] / jnp.maximum(dc, 1.0)) * nc

    def far_setup(qb):
        for j in range(PICKS):
            spread(blk[slots[0, qb * PICKS + j] & 63], j * KBLK, 32, se, so, sx)
        rs = iota((QBLK, 128), 0)
        cs = iota((QBLK, 128), 1)
        bs[...] = jnp.where((cs < 64) & (cs > rs), DEAD, jnp.broadcast_to(rowb[qb][0:1, :128], (QBLK, 128)))

    def far(qb):
        base = pl.multiple_of(qb * QBLK, QBLK)
        r = pl.ds(base, QBLK)
        top = pl.ds(pl.multiple_of(core * 128, 128), 128)
        low = pl.ds(pl.multiple_of(128 - core * 128, 128), 128)
        for h in range(8):
            off = (h // 2) * 384 + (h % 2) * 128
            ns, ds = named_branch(
                q[r, off : off + 256], (so if h % 2 else se)[...], sx[...], bs[...], rowb[qb][0:1, 128:]
            )
            c = slice(h * DV, (h + 1) * DV)
            y = (acc[r, c] + accc[r, c] + (gt[r, 8 + h : 9 + h] / ds) * ns).astype(BF)
            att[top, c] = y[:128]
            att[low, c] = y[128:]

    def pr(r, c):
        return remote(psend.at[r, c], precv.at[r, c], pr_s.at[r, c], pr_r.at[r, c], sib)

    def project(r):
        def side(i):
            c = jnp.where(r == 1, 1 - i, i)
            y = jnp.dot(att[...], w[:, pl.ds(pl.multiple_of(c * HALF, 128), HALF)], preferred_element_type=F32)
            psend[r, c] = y[128:].astype(BF)
            pr(r, c).start()
            mine[r, c] = y[:128]

        each(0, 2, side)

    A, B = 0, 1

    def total(r, c):
        pr(r, c).wait_recv()
        return mine[r, c] + precv[r, c].astype(F32)

    def hop_a(k):
        return remote(sa.at[k], ra.at[k], a_s.at[k], a_r.at[k], up)

    def hop_b(k):
        return remote(sb.at[k], rb.at[k], b_s.at[k], b_r.at[k], down)

    def block_of(r):
        return (x + jnp.where(r == 0, 2, jnp.where(r == 1, 1, jnp.where(r == 2, 3, 0)))) % 4

    def late(k):
        return jnp.where(x >= 3 - k, 2 - k, 3 - k)

    def ship0():
        sa[0] = total(0, A).astype(BF)
        hop_a(0).start()
        sb[0] = total(0, B).astype(BF)
        hop_b(0).start()

    def ship1():
        sa[1] = total(1, B).astype(BF)
        hop_a(1).start()
        own = total(1, A)
        hop_a(0).wait_recv()
        sa[2] = (own + ra[0].astype(F32)).astype(BF)
        hop_a(2).start()

    def ship2():
        sb[1] = total(2, A).astype(BF)
        hop_b(1).start()

    def ship3():
        own = total(2, B)
        hop_b(0).wait_recv()
        sb[2] = (own + rb[0].astype(F32)).astype(BF)
        hop_b(2).start()

    cut1 = jnp.where(me % 4 == 0, me, 2 * (me // 3))
    cut2 = jnp.where(me % 4 == 0, me, me // 3)
    early = (me % 4 == 0) & (me > 0) & (x >= 2)

    def go(i):
        is_w = (i <= 2) | ((i == 3) & early) | ((i == 10) & jnp.logical_not(early))
        is_c = ((i >= 4) & (i <= 6)) | (i == 11)
        is_f = ((i >= 7) & (i <= 9)) | (i == 12)
        w_block = jnp.where(
            (i == 10) | ((i == 1) & early), x, late(jnp.where(early & (i >= 2), i - 1, i))
        )
        c_block = jnp.where(i == 11, x, late(i - 4))
        r = jnp.where(i == 12, 3, i - 7)

        @pl.when(i == 4)
        def _():
            each(1, me + 1, lambda d: cp_in(d).wait_recv())
            for k in range(16):
                spread(comp[k], k * CBLK, 16, ce, co, cx)

        @pl.when(i == jnp.where((x >= 2) & jnp.logical_not(early), 1, 2))
        def _():
            @pl.when(me > 0)
            def _():
                rim_c.wait_recv()
                rim_f.start()

            @pl.when(me > 0)
            def _():
                rim_f.wait_recv()

            for j in range(8):
                spread(rim[j], j * KBLK, 32, ke, ko, vx)

        @pl.when(i == 5)
        def _():
            each(cut1, me, pass_on)

        @pl.when(i == 6)
        def _():
            each(cut2, cut1, pass_on)

        @pl.when(i == 7)
        def _():
            each(0, cut2, pass_on)
            loads[7].wait()
            to_s.wait()
            each(0, me, lambda o: fw_in(o).wait_recv())

        @pl.when(is_w)
        def _():
            window(w_block)

        @pl.when(i == 0)
        def _():
            each(me + 1, n, take)
            each(me + 1, n, give)

        @pl.when(is_c)
        def _():
            compressed(c_block)

        @pl.when(is_f)
        def _():
            far_setup(block_of(r))

            @pl.when(i == 8)
            def _():
                ship0()

            @pl.when(i == 9)
            def _():
                ship1()

            far(block_of(r))
            project(r)

        @pl.when(i == 9)
        def _():
            ship2()

        @pl.when(i == 10)
        def _():
            ship3()

    each(0, 13, go)
    own_a = total(3, A)
    hop_a(2).wait_recv()
    hop_b(1).wait_recv()
    outb[:, :HALF] = (own_a + ra[2].astype(F32) + rb[1].astype(F32)).astype(BF)
    own_b = total(3, B)
    hop_a(1).wait_recv()
    hop_b(2).wait_recv()
    outb[:, HALF:] = (own_b + ra[1].astype(F32) + rb[2].astype(F32)).astype(BF)
    done = pltpu.make_async_copy(outb, o_hbm, lsem.at[9])
    done.start()

    each(0, me, lambda o: rq(o).wait_send())
    each(me + 1, n, lambda t: cp(t).wait_send())
    each(me + 1, n, lambda t: bk(t).wait_send())
    each(0, me, lambda o: fw(o).wait_send())

    @pl.when(me < n - 1)
    def _():
        rim_c.wait_send()

    @pl.when(me > 0)
    def _():
        rim_f.wait_send()

    for r in range(4):
        pr(r, A).wait_send()
        pr(r, B).wait_send()
    for k in range(3):
        hop_a(k).wait_send()
        hop_b(k).wait_send()
    done.wait()


def local(queries, key_rows, value_rows, kw, vw, picks, gate, w):
    hbm = pl.BlockSpec(memory_space=pl.ANY)
    V = pltpu.VMEM
    D = pltpu.SemaphoreType.DMA
    return pl.pallas_call(
        layer,
        in_specs=[hbm] * 8,
        out_specs=hbm,
        out_shape=jax.ShapeDtypeStruct((128, 2560), BF),
        scratch_shapes=[
            V((1024, 1536), BF), V((1024, 384), BF), V((1024, DV), BF), V((CBLK, 384), F32), V((CBLK, DV), F32),
            V((4, 4, PICKS), I32), V((24, 1024), F32), V((1024, 2560), BF), V((1024, 128), F32),
            V((16, 32, 640), BF), V((32, 384), F32), V((16, 640), BF), V((8, 128), I32), V((16, 8, 128), I32),
            pltpu.SMEM((16, 8, 128), I32), V((8, 128), I32), pltpu.SMEM((8, 128), I32),
            V((16, 2, 32, 640), BF), V((64, 32, 640), BF), V((16, 16, 640), BF), V((8, 32, 640), BF),
            V((1536, 256), BF), V((1536, 256), BF), V((1536, 256), BF),
            V((512, 256), BF), V((512, 256), BF), V((512, 256), BF),
            V((1024, 256), BF), V((1024, 256), BF), V((1024, 256), BF),
            V((QBLK, 768), F32), V((QBLK, 512), F32), V((QBLK, 128), F32), V((4, 8, 1024), F32),
            V((1024, 1024), F32), V((1024, 1024), F32), V((QBLK, 1024), BF),
            V((4, 2, 128, HALF), F32), V((4, 2, 128, HALF), BF), V((4, 2, 128, HALF), BF),
            V((3, 128, HALF), BF), V((3, 128, HALF), BF), V((3, 128, HALF), BF), V((3, 128, HALF), BF),
            V((128, 2560), BF),
            D((10,)), D((16,)), D((16,)), D((16,)), D((2,)), D((2,)), D((16,)), D((16,)), D((16,)), D((16,)), D((16,)), D((16,)),
            D((4, 2)), D((4, 2)), D((3,)), D((3,)), D((3,)), D((3,)),
        ],
        compiler_params=pltpu.CompilerParams(
            collective_id=0, has_side_effects=True, vmem_limit_bytes=60 << 20
        ),
    )(queries, key_rows, value_rows, kw, vw, picks, gate.transpose(1, 2, 0).reshape(24, 1024), w)


def solution(mesh):
    placed = (
        P("ctx", "head"), P("ctx", None), P("ctx", None), P(), P(),
        P("ctx", None, None), P("ctx", None, "head"), P("head", None),
    )
    return jax.shard_map(
        local, mesh=mesh, in_specs=placed, out_specs=P(("ctx", "head"), None), check_vma=False
    )
```
